128 devices in a mesh: flow: 32 (over z, x, core), grp: 4 (over y).
Axes of the slice: x: 4, y: 4, z: 4, core: 2. Of those that a mesh axis runs over, the one named last changes fastest.
Arguments:
- velocity: float32 [3, 256, 32, 128], P(None, 'flow', 'grp'), may hold values from -6 to 6
- column_slot: int32 [256, 32], P('flow', 'grp'), may hold values from 0 to 2047, as said below
- scalars: float32 [32, 1048576], P(None, ('flow', 'grp')), may hold values from -6 to 6
- mass: float32 [1048576], P(('flow', 'grp')), may hold values from 0.5 to 2
- pair_weight: float32 [1048576], P(('flow', 'grp')), may hold values from 0.25 to 2
- particle_cell: int32 [1048576], P(('flow', 'grp')), may hold values from 0 to 8191
- mix_partner: int32 [1048576], P(('flow', 'grp')), may hold values from 0 to 8191
- migrate_to: int32 [1048576, 1], P(('flow', 'grp')), may hold values from 0 to 31; in each aligned block of 8192 rows (0 to 8191, 8192 to 16383, ...) at most 512 rows name the same one
- rate_matrix: float32 [32, 32], replicated, may hold values from -1 to 1
- enthalpy: float32 [32], replicated, may hold values from -1 to 1
Outputs:
- cell_energy: float32 [256, 32, 128], P('flow', 'grp')
- cell_density: float32 [256, 32, 128], P('flow', 'grp')
- moved_scalars: float32 [32, 2097152], P(None, ('flow', 'grp'))
- moved_mass: float32 [2097152], P(('flow', 'grp'))
The draws below stay inside these ranges and needn't reach their ends.
Inputs may be any that keep to these rules, and one draw needn't show every extreme that they name: `column_slot`: for each grp index g the values of the columns y with y // 8 == g form a permutation of 0 to 2047. The 64 columns of one device send at most 4 columns to one partition v // 64, and some device sends exactly 4 to some partition in every draw. `particle_cell`: index into the cells of the particle's own device, position * 128 + z. `mix_partner`: index of the partner among the particles of the same device. `migrate_to`: among the 8192 particles of one device at most 512 name one partition, and that bound is reached in every draw.
All inputs are finite; a program needn't handle non-finite values.
Results may differ from the reference program's by a relative error of at most 0.0003.
Values sent between devices are 32-bit elements; how exact they have to be, the bound alone decides.
A program may use at most 64 MiB of HBM per device.

```python
import math
import jax
import jax.numpy as jnp
import numpy as np
from jax import lax

S = 32
CX = 8
CY = 8
NZ = 128
P_DEV = 8192
NB_DEV = 64
MOST = 512
NX = 256
NY = 32
P_ALL = 1048576
M_ALL = 2097152
N_FLOW = 32
N_GRP = 4
DEVICES = 128


def slot_group(key):
    half = NB_DEV // N_FLOW
    keys = jax.random.split(key, 5)
    order = jax.random.permutation(keys[0], N_FLOW)
    amounts = jax.random.randint(keys[1], (N_FLOW // 2,), 0, half + 1)
    amounts = amounts.at[0].set(half)
    multiple = jnp.full((N_FLOW,), half, jnp.int32)
    multiple = multiple.at[order[0::2]].add(amounts).at[order[1::2]].add(-amounts)
    shuffle = jax.random.permutation(keys[2], N_FLOW)
    source = jnp.arange(N_FLOW, dtype=jnp.int32)[:, None]
    partner = jnp.arange(N_FLOW, dtype=jnp.int32)[None, :]
    counts = multiple[(shuffle[partner] - source) % N_FLOW]
    ends = jnp.cumsum(counts, axis=1)
    steps = jnp.arange(NB_DEV, dtype=jnp.int32)
    target = jnp.sum((ends[:, None, :] <= steps[None, :, None]).astype(jnp.int32), axis=2)
    starts = jnp.take_along_axis(ends - counts, target, axis=1)
    rank = steps[None, :] - starts
    column_start = jnp.cumsum(counts, axis=0) - counts
    offset = jnp.take_along_axis(column_start, target, axis=1) + rank
    perms = jax.vmap(lambda k: jax.random.permutation(k, NB_DEV))(jax.random.split(keys[3], N_FLOW))
    position = perms[target, offset]
    value = target * NB_DEV + position
    column_perm = jax.vmap(lambda k: jax.random.permutation(k, NB_DEV))(jax.random.split(keys[4], N_FLOW))
    return jnp.take_along_axis(value, column_perm, axis=1)


def draw_column_slot(key, part):
    base = jax.random.fold_in(key, 11)
    values = jax.vmap(slot_group)(jax.random.split(base, N_GRP))
    values = values.reshape(N_GRP, N_FLOW, CX, CY)
    return jnp.transpose(values, (1, 2, 0, 3)).reshape(NX, NY).astype(jnp.int32)


def with_ends(drawn, rng, low, largest):
    longest = drawn.shape.index(max(drawn.shape))
    spots = []
    for shift in (0, 1):
        where = [jax.random.randint(jax.random.fold_in(rng, axis), (), 0, length) for axis, length in enumerate(drawn.shape)]
        where[longest] = (where[longest] + shift) % drawn.shape[longest]
        spots.append(tuple(where))
    return drawn.at[spots[0]].set(low).at[spots[1]].set(largest)


def level_of(rng, extent, cuts, smallest, top_value):
    gain, own = 1.0, jax.random.fold_in(rng, 6)
    for dim, shards_of in cuts:
        heights = jnp.exp(jax.random.uniform(jax.random.fold_in(own, dim), (shards_of,), jnp.float32, smallest / len(cuts), top_value / len(cuts)))
        gain = gain * jnp.repeat(heights, extent[dim] // shards_of).reshape([-1 if axis == dim else 1 for axis in range(len(extent))])
    return gain


def routed_block(rng, own, number, rows, count, top, reach, skew):
    ranking = jax.random.permutation(rng, count)
    heavy_load, ordinary = portions_of(count, rows * top, reach, skew, True), portions_of(count, rows * top, reach, skew, False)
    places = jnp.arange(count)

    def named(lengths, turn):
        used = int((lengths > 0).sum())
        fixed = max(1, used // 4)
        passed = fixed + (places - fixed + turn * (used - fixed)) % max(1, count - fixed)
        return jnp.zeros((count,), jnp.int32).at[ranking[jnp.where(places < fixed, places, passed)]].set(jnp.asarray(lengths, jnp.int32))

    lengths = jnp.where(number % 4 == 0, named(heavy_load, number // 4), named(ordinary, number - number // 4 - 1))
    mixed = jax.random.permutation(jax.random.fold_in(own, 3), count)
    giver, receiver = mixed[0:count // 2 * 2:2], mixed[1:count // 2 * 2:2]
    margin = jnp.minimum(lengths[giver] - 1, reach - lengths[receiver]) // 2
    margin = jnp.where((giver == ranking[0]) | (receiver == ranking[0]) | (lengths[receiver] == 0), 0, jnp.maximum(margin, 0))
    passed = jax.random.randint(jax.random.fold_in(own, 4), (count // 2,), 0, 1 << 20) % (margin + 1)
    lengths = lengths.at[giver].add(-passed).at[receiver].add(passed)
    items = jnp.searchsorted(jnp.cumsum(lengths), jnp.arange(rows * top), side="right").astype(jnp.int32)
    table = items.reshape(top, rows).T
    table = table[jax.random.permutation(jax.random.fold_in(own, 1), rows)]
    turn = jax.random.randint(jax.random.fold_in(own, 2), (rows, 1), 0, top)
    return jnp.take_along_axis(table, (jnp.arange(top)[None, :] + turn) % top, axis=1)


def portions_of(count, total, limit, lean, full):
    loads = [(1 << 20) // math.isqrt(standing ** lean) + 1 for standing in range(1, count + 1)]
    largest = limit if full else min(limit, max(-(-total // count), total * loads[0] // sum(loads)))
    least = 1 if total - largest >= count - 1 else 0
    holding, surplus = [largest] + [least] * (count - 1), total - largest - least * (count - 1)
    while surplus > 0:
        movable = [i for i in range(1, count) if holding[i] < largest] or [i for i in range(1, count) if holding[i] < limit]
        whole, remaining = sum([loads[i] for i in movable]), surplus
        for i in movable:
            extra = min(limit - holding[i], max(1, remaining * loads[i] // whole), surplus)
            holding[i] = holding[i] + extra
            surplus = surplus - extra
    return np.array(holding)


def bell_draw(own_key, extent, width, bound, cuts=(), kind=jnp.bfloat16):
    drawn = width * jax.random.normal(own_key, extent, jnp.float32)
    if cuts:
        drawn = drawn * level_of(own_key, extent, cuts, -0.22, 0.18)
    return jnp.clip(drawn, -bound, bound).astype(kind)


def setup_inputs(seed: int = 0) -> dict:
    seeds = jax.random.split(jax.random.key(seed), 11)
    velocity = bell_draw(seeds[0], (3, NX, NY, NZ), 1.0, 6.0, ((1, 32), (2, 4)), jnp.float32)
    column_slot = draw_column_slot(jax.random.fold_in(seeds[10], 71), 0)
    scalars = bell_draw(seeds[2], (S, P_ALL), 1.0, 6.0, ((1, 128),), jnp.float32)
    mass = jnp.clip(jnp.exp(math.log(2.0) - 1.3862944 * jax.random.uniform(seeds[3], (P_ALL,), jnp.float32) ** level_of(seeds[3], (P_ALL,), ((0, 128),), -0.2, 0.2)), 0.5, 2.0)
    pair_weight = jnp.clip(0.25 + 1.75 * jax.random.uniform(seeds[4], (P_ALL,), jnp.float32) ** level_of(seeds[4], (P_ALL,), ((0, 128),), -0.2, 0.2), 0.25, 2.0)
    particle_cell = with_ends(jax.random.randint(seeds[5], (P_ALL,), 0, CX * CY * NZ), jax.random.fold_in(seeds[5], 1), 0, (CX * CY * NZ) - 1).astype(jnp.int32)
    mix_partner = with_ends(jax.random.randint(seeds[6], (P_ALL,), 0, P_DEV), jax.random.fold_in(seeds[6], 1), 0, P_DEV - 1).astype(jnp.int32)
    migrate_to_keys = jax.random.split(jax.random.fold_in(seeds[7], 1), P_ALL // P_DEV)
    migrate_to_turns = jax.random.permutation(jax.random.fold_in(seeds[7], 3), P_ALL // P_DEV)
    migrate_to = jax.vmap(lambda own, number: routed_block(jax.random.fold_in(seeds[7], 2), own, number, P_DEV, N_FLOW, 1, MOST, 2))(migrate_to_keys, migrate_to_turns).reshape((P_ALL, 1))
    rate_matrix = bell_draw(seeds[8], (S, S), S ** -0.5, 1.0, (), jnp.float32)
    enthalpy = bell_draw(seeds[9], (S,), S ** -0.5, 1.0, (), jnp.float32)
    return {"velocity": velocity, "column_slot": column_slot, "scalars": scalars, "mass": mass, "pair_weight": pair_weight, "particle_cell": particle_cell, "mix_partner": mix_partner, "migrate_to": migrate_to, "rate_matrix": rate_matrix, "enthalpy": enthalpy}


mix_step = 0.5
react_step = 0.5

def strain_omega(velocity):
    padded = jnp.pad(velocity, ((0, 0), (1, 1), (1, 1), (1, 1)))
    diff_x = padded[:, 2:, 1:-1, 1:-1] - padded[:, :-2, 1:-1, 1:-1]
    diff_y = padded[:, 1:-1, 2:, 1:-1] - padded[:, 1:-1, :-2, 1:-1]
    diff_z = padded[:, 1:-1, 1:-1, 2:] - padded[:, 1:-1, 1:-1, :-2]
    strain = lax.optimization_barrier(jnp.sum(diff_x * diff_x + diff_y * diff_y + diff_z * diff_z, axis=0)) * 0.25
    return 0.5 + 0.25 * jnp.sqrt(strain)

def exclusive_rank(labels, count):
    onehot = (labels[:, None] == jnp.arange(count, dtype=jnp.int32)[None, :]).astype(jnp.int32)
    before = jnp.cumsum(onehot, axis=0) - onehot
    return lax.optimization_barrier(jnp.sum(before * onehot, axis=1)).astype(jnp.int32)

def reference(velocity, column_slot, scalars, mass, pair_weight, particle_cell, mix_partner, migrate_to, rate_matrix, enthalpy):
    omega = strain_omega(velocity)
    kinetic = 0.5 * lax.optimization_barrier(jnp.sum(velocity * velocity, axis=0))
    partition = column_slot // NB_DEV
    position = column_slot % NB_DEV
    group_of = (jnp.arange(NY, dtype=jnp.int32) // CY)[None, :]
    target = ((partition * N_GRP + group_of) * NB_DEV + position).reshape(-1).astype(jnp.int32)
    stacked = jnp.stack([omega, kinetic]).reshape(2, NX * NY, NZ)
    placed = jnp.zeros((2, DEVICES * NB_DEV, NZ), jnp.float32).at[:, target].set(stacked)
    placed = placed.reshape(2, DEVICES, NB_DEV * NZ)
    cell_rows = particle_cell.reshape(DEVICES, P_DEV)
    at_cell = jnp.take_along_axis(placed, cell_rows[None], axis=2).reshape(2, P_ALL)
    omega_part = at_cell[0]
    kinetic_part = at_cell[1]
    device_of = jnp.arange(P_ALL, dtype=jnp.int32) // P_DEV
    partner_index = (device_of * P_DEV + mix_partner).astype(jnp.int32)
    partner = jnp.take(scalars, partner_index, axis=1)
    fraction = 1.0 - jnp.exp(-mix_step * pair_weight * omega_part)
    mixed = scalars + fraction[None, :] * (partner - scalars)
    rate = jnp.dot(rate_matrix, mixed, precision=lax.Precision.HIGHEST)
    reacted = mixed + react_step * jnp.tanh(rate)
    energy = jnp.dot(enthalpy, reacted, precision=lax.Precision.HIGHEST) + kinetic_part
    bin_index = (device_of * (NB_DEV * NZ) + particle_cell).astype(jnp.int32)
    density = jax.ops.segment_sum(mass, bin_index, num_segments=DEVICES * NB_DEV * NZ)
    energy_sum = jax.ops.segment_sum(mass * energy, bin_index, num_segments=DEVICES * NB_DEV * NZ)
    cell_energy = energy_sum.reshape(DEVICES * NB_DEV, NZ)[target].reshape(NX, NY, NZ)
    cell_density = density.reshape(DEVICES * NB_DEV, NZ)[target].reshape(NX, NY, NZ)
    target_part = migrate_to[:, 0]
    move_rank = lax.map(lambda row: exclusive_rank(row, N_FLOW), target_part.reshape(DEVICES, P_DEV)).reshape(P_ALL)
    source_flow = device_of // N_GRP
    source_grp = device_of % N_GRP
    slot = (((target_part * N_GRP + source_grp) * N_FLOW + source_flow) * MOST + move_rank).astype(jnp.int32)
    moved_scalars = jnp.zeros((S, M_ALL), jnp.float32).at[:, slot].set(reacted)
    moved_mass = jnp.zeros((M_ALL,), jnp.float32).at[slot].set(mass)
    return (cell_energy, cell_density, moved_scalars, moved_mass)
```

```python
import functools

import jax
import jax.numpy as jnp
from jax import lax
from jax.experimental import pallas as pl
from jax.experimental.pallas import tpu as pltpu
from jax.sharding import PartitionSpec as P

mix_step = 0.5
react_step = 0.5
MESH = pl.DeviceIdType.MESH
f32 = jnp.float32
bf16 = jnp.bfloat16
i32 = jnp.int32
HIGH = lax.Precision.HIGHEST

N = 32
NG = 4
PD = 8192
CH = PD // 128
CAP = 512
COLS = 64

_GROUPS = [
    [(2, 2)],
    [(1, 2), (3, 2), (2, 1), (2, 3)],
    [(1, 3), (3, 1)],
    [(1, 1), (3, 3)],
    [(0, 2), (2, 0)],
    [(0, 1), (0, 3), (1, 0), (3, 0)],
]
_ORDER = [(a, b, c) for g in _GROUPS for c in (0, 1) for (a, b) in g] + [(0, 0, 1)]
_CODES = [a * 8 + b * 2 + c for (a, b, c) in _ORDER]
_WORDS = [
    sum(code << (5 * j) for j, code in enumerate(_CODES[6 * w : 6 * w + 6]))
    for w in range(6)
]


def ordered_peer(t, me):
    w = t // 6
    word = jnp.int32(_WORDS[0])
    for j in range(1, 6):
        word = jnp.where(w == j, jnp.int32(_WORDS[j]), word)
    code = jnp.bitwise_and(jnp.right_shift(word, 5 * (t - 6 * w)), 31)
    z = lax.rem(me // 8 + code // 8, 4)
    x = lax.rem(lax.rem(me // 2, 4) + lax.rem(code // 2, 4), 4)
    c = lax.rem(me + code, 2)
    return (z * 4 + x) * 2 + c


def split2(x):
    hi = x.astype(bf16)
    lo = (x - hi.astype(f32)).astype(bf16)
    return hi, lo


def split3(x):
    hi = x.astype(bf16)
    r = x - hi.astype(f32)
    mid = r.astype(bf16)
    lo = (r - mid.astype(f32)).astype(bf16)
    return hi, mid, lo


def dot(a, b):
    return jnp.dot(a, b, preferred_element_type=f32)


def dot_nt(a, b):
    return lax.dot_general(a, b, (((1,), (1,)), ((), ())), preferred_element_type=f32)


def select_dot(hot, x):
    a, b, c = split3(x)
    return dot(hot, a) + dot(hot, b) + dot(hot, c)


def iota(shape, dim):
    return lax.broadcasted_iota(i32, shape, dim)


def kernel(
    vel_in, vrow_in, scal_in, mass_in, pw_in, cell_in, mig_in, part, rmat_in, enth_in,
    ce, cd, ms, mm,
    vel, vrow, scal, mass, pw, cell, mig, rmat, enth,
    hx, hy, ysnd, ypad, q2, q2t, wmat, possend, posrecv, fsend, frecv, bsend, brecv,
    rows, pt, gbuf, slot, srcv, mbuf, tab, frac, kinp, en, sendbuf,
    part_s, src_s,
    isem, lsem, hss, hrs, pss, prs, css, crs, mss, mrs, dss, drs, bss, brs,
):
    me = lax.axis_index("flow")
    g = lax.axis_index("grp")

    def peer(t):
        return lax.rem(me + t, N)

    loads = [
        pltpu.make_async_copy(src, dst, isem.at[k])
        for k, (src, dst) in enumerate(
            [
                (vrow_in, vrow), (vel_in, vel), (scal_in, scal), (mig_in, mig), (mass_in, mass),
                (pw_in, pw), (cell_in, cell), (rmat_in, rmat), (enth_in, enth), (part, part_s),
            ]
        )
    ]
    for copy in loads:
        copy.start()

    def remote(src, dst, ss, rs, dev):
        return pltpu.make_async_remote_copy(
            src_ref=src, dst_ref=dst, send_sem=ss, recv_sem=rs, device_id=dev, device_id_type=MESH
        )

    barrier = pltpu.get_barrier_semaphore()

    def greet(t, _):
        pl.semaphore_signal(barrier, inc=1, device_id=(peer(t), g), device_id_type=MESH)
        return 0

    lax.fori_loop(1, N, greet, 0)
    for s in (1, NG - 1):
        pl.semaphore_signal(
            barrier, inc=1, device_id=(me, lax.rem(g + s, NG)), device_id_type=MESH
        )
    loads[0].wait()

    v = vrow[0:1, :]
    lane1 = iota((1, 128), 1)
    field = jnp.right_shift(lane1, 6)
    target = jnp.right_shift(v, 6)
    place = jnp.bitwise_and(v, 63) + 64 * field
    key = jnp.broadcast_to((target + 64 * field).astype(f32), (128, 128))
    earlier = jnp.where(
        jnp.logical_and(key.T == key, iota((128, 128), 0) < iota((128, 128), 1)), 1.0, 0.0
    )
    rank = jnp.sum(earlier, axis=0, keepdims=True).astype(i32)
    sidx = target * 8 + field * 4 + rank
    q2v = jnp.where(iota((256, 128), 0) == sidx, 1.0, 0.0).astype(bf16)
    q2[...] = q2v
    sidx_t = jnp.broadcast_to(sidx.astype(f32), (128, 128)).T.astype(i32)
    for h in range(2):
        q2t[:, 128 * h : 128 * h + 128] = jnp.where(
            iota((128, 128), 1) + 128 * h == sidx_t, 1.0, 0.0
        ).astype(bf16)
    place_t = jnp.broadcast_to((place + 1).astype(f32), (128, 128)).T.astype(bf16)
    possend[...] = dot(q2v, place_t) - 1.0
    loads[1].wait()
    for c in range(3):
        for x in range(8):
            ysnd[0, c, x : x + 1, :] = vel[c, x, 0:1, :]
            ysnd[1, c, x : x + 1, :] = vel[c, x, 7:8, :]

    pl.semaphore_wait(barrier, N - 1 + 2)

    nxt, prv = lax.rem(me + 1, N), lax.rem(me + N - 1, N)
    gn, gp = lax.rem(g + 1, NG), lax.rem(g + NG - 1, NG)
    halo = [
        remote(vel.at[:, 7], hx.at[0], hss.at[0], hrs.at[0], (nxt, g)),
        remote(vel.at[:, 0], hx.at[1], hss.at[1], hrs.at[1], (prv, g)),
        remote(ysnd.at[1], hy.at[0], hss.at[2], hrs.at[2], (me, gn)),
        remote(ysnd.at[0], hy.at[1], hss.at[3], hrs.at[3], (me, gp)),
    ]
    for copy in halo:
        copy.start()

    def rows8(d):
        return pl.ds(pl.multiple_of(d * 8, 8), 8)

    def exchange(src, dst, ss, rs, own):
        def send(t, _):
            p = peer(t)
            remote(src.at[rows8(p)], dst.at[rows8(me)], ss.at[p], rs.at[me], (p, g)).start()
            return 0

        lax.fori_loop(1, N, send, 0)
        pltpu.make_async_copy(src.at[rows8(me)], dst.at[rows8(me)], own).start()

    def arrive(src, dst, ss, rs, own):
        def done(t, _):
            p = peer(t)
            copy = remote(src.at[rows8(p)], dst.at[rows8(p)], ss.at[p], rs.at[p], (p, g))
            copy.wait_send()
            copy.wait_recv()
            return 0

        lax.fori_loop(1, N, done, 0)
        pltpu.make_async_copy(src.at[rows8(me)], dst.at[rows8(me)], own).wait()

    exchange(possend, posrecv, pss, prs, lsem.at[1])

    loads[2].wait()

    def to_rows(c, _):
        col = pl.ds(pl.multiple_of(c * 128, 128), 128)
        x = scal[:, col]
        rows[col, :] = jnp.concatenate([x, x, x, x], axis=0).T
        return 0

    lax.fori_loop(0, CH // 2, to_rows, 0, unroll=8)

    for copy in halo:
        copy.wait()
    strain = jnp.zeros((64, 128), f32)
    square = jnp.zeros((64, 128), f32)
    lane64 = iota((64, 128), 1)
    for c in range(3):
        a = vel[c]
        left = jnp.where(me == 0, 0.0, hx[0, c])
        right = jnp.where(me == N - 1, 0.0, hx[1, c])
        down = jnp.where(g == 0, 0.0, hy[0, c])
        up = jnp.where(g == NG - 1, 0.0, hy[1, c])
        dx = jnp.concatenate([a[1:], right[None]], axis=0) - jnp.concatenate(
            [left[None], a[:-1]], axis=0
        )
        for x in range(8):
            ypad[x, 7:8, :] = down[x : x + 1, :]
            ypad[x, 8:16, :] = a[x]
            ypad[x, 16:17, :] = up[x : x + 1, :]
        dy = ypad[:, 9:17, :] - ypad[:, 7:15, :]
        flat = a.reshape(64, 128)
        dz = jnp.where(lane64 == 127, 0.0, pltpu.roll(flat, 127, 1)) - jnp.where(
            lane64 == 0, 0.0, pltpu.roll(flat, 1, 1)
        )
        dx = dx.reshape(64, 128)
        dy = dy.reshape(64, 128)
        strain = strain + (dx * dx + dy * dy + dz * dz)
        square = square + flat * flat
    omega = 0.5 + 0.25 * jnp.sqrt(strain * 0.25)
    both = jnp.concatenate([omega, 0.5 * square], axis=0)
    fsend[...] = select_dot(q2[...], both)
    exchange(fsend, frecv, css, crs, lsem.at[2])

    lax.fori_loop(CH // 2, CH, to_rows, 0, unroll=8)

    for copy in loads[3:9]:
        copy.wait()

    tri = jnp.concatenate(
        [
            jnp.where(iota((128, 128), 0) < iota((128, 128), 1), 1.0, 0.0).astype(bf16),
            jnp.ones((128, 128), bf16),
        ],
        axis=1,
    )

    def ranks(b, carry):
        hots = []
        for j in range(8):
            p = mig[pl.ds(b * 8 + j, 1), :]
            hots.append(jnp.where(iota((32, 128), 0) == p, 1.0, 0.0))
        hot = jnp.concatenate(hots, axis=0)
        pre = dot(hot.astype(bf16), tri)
        out = []
        for j in range(8):
            sl = slice(32 * j, 32 * j + 32)
            out.append(
                jnp.sum(hots[j] * (pre[sl, :128] + carry), axis=0, keepdims=True).astype(i32)
            )
            carry = carry + pre[sl, 128:]
        r8 = pl.ds(pl.multiple_of(b * 8, 8), 8)
        slot[r8, :] = mig[r8, :] * CAP + jnp.concatenate(out, axis=0)
        return carry

    lax.fori_loop(0, 8, ranks, jnp.zeros((32, 128), f32))

    def inverse(b, acc):
        left, right = [], []
        sub = iota((128, 128), 0)
        for j in range(4):
            c = b * 4 + j
            s = slot[pl.ds(c, 1), :]
            m = mass[pl.ds(c, 1), :]
            m_hi = m.astype(bf16).astype(f32)
            m_lo = m - m_hi
            left.append(jnp.where(sub == jnp.right_shift(s, 7), 1.0, 0.0).astype(bf16))
            at = sub == jnp.bitwise_and(s, 127)
            code = PD - c * 128 - lane1
            hi = jnp.right_shift(code, 7).astype(f32)
            lo = jnp.bitwise_and(code, 127).astype(f32)
            right.append(
                jnp.concatenate(
                    [jnp.where(at, w, 0.0).astype(bf16) for w in (hi, lo, m_hi, m_lo)], axis=0
                )
            )
        return acc + dot_nt(jnp.concatenate(left, axis=1), jnp.concatenate(right, axis=1))

    inv = lax.fori_loop(0, CH // 4, inverse, jnp.zeros((128, 512), f32))
    srcv[...] = jnp.clip((PD - (inv[:, 0:128] * 128.0 + inv[:, 128:256])).astype(i32), 0, PD)
    moved = inv[:, 256:384] + inv[:, 384:512]
    for p in range(N):
        mbuf[p] = moved[4 * p : 4 * p + 4, :]
    loads[9].wait()

    lanes = iota((1, 128), 1)
    quarter = [lanes < 32, lanes < 64, lanes < 96]

    def packed(index):
        a, b, c, d = [rows[pl.ds(index(q), 1), :] for q in range(4)]
        return jnp.where(quarter[1], jnp.where(quarter[0], a, b), jnp.where(quarter[2], c, d))

    def partners(b, _):
        for r in range(128):
            gbuf[r : r + 1, :] = packed(lambda q: part_s[4 * b + q, r])
        t = gbuf[...].T
        for q in range(4):
            col = pl.ds(pl.multiple_of(b * 512 + q * 128, 128), 128)
            pt[:, col] = t[32 * q : 32 * q + 32, :]
        return 0

    lax.fori_loop(0, 16, partners, 0)

    src_copy = pltpu.make_async_copy(srcv, src_s, lsem.at[3])
    src_copy.start()

    def send_mass(t, _):
        p = peer(t)
        remote(mbuf.at[p], mm.at[me], mss.at[p], mrs.at[me], (p, g)).start()
        return 0

    lax.fori_loop(1, N, send_mass, 0)
    own_mass = pltpu.make_async_copy(mbuf.at[me], mm.at[me], lsem.at[4])
    own_mass.start()

    arrive(possend, posrecv, pss, prs, lsem.at[1])
    pos = posrecv[...]
    wmat[...] = jnp.where(pos == iota((256, 128), 1).astype(f32), 1.0, 0.0).astype(bf16)
    wt = jnp.where(pos.T == iota((128, 256), 0).astype(f32), 1.0, 0.0).astype(bf16)
    arrive(fsend, frecv, css, crs, lsem.at[2])
    tab[...] = select_dot(wt, frecv[...])

    cz = [jnp.bitwise_and(cell[8 * k : 8 * k + 8, :], 127) for k in range(8)]
    cp = [jnp.right_shift(cell[8 * k : 8 * k + 8, :], 7) for k in range(8)]

    def lookup(n, acc):
        om = jnp.broadcast_to(tab[pl.ds(n, 1), :], (8, 128))
        ki = jnp.broadcast_to(tab[pl.ds(n + 64, 1), :], (8, 128))
        out = []
        for k in range(8):
            here = cp[k] == n
            out.append(jnp.where(here, jnp.take_along_axis(om, cz[k], axis=1), acc[2 * k]))
            out.append(jnp.where(here, jnp.take_along_axis(ki, cz[k], axis=1), acc[2 * k + 1]))
        return tuple(out)

    found = lax.fori_loop(0, 64, lookup, tuple(jnp.zeros((8, 128), f32) for _ in range(16)))
    for k in range(8):
        sl = slice(8 * k, 8 * k + 8)
        frac[sl, :] = 1.0 - jnp.exp(-mix_step * pw[sl, :] * found[2 * k])
        kinp[sl, :] = found[2 * k + 1]

    rates = rmat[...]
    forms = jnp.broadcast_to(enth[...], (8, 32))

    def react(b, _):
        mixed = []
        for j in range(4):
            c = b * 4 + j
            col = pl.ds(pl.multiple_of(c * 128, 128), 128)
            s = scal[:, col]
            mixed.append(s + frac[pl.ds(c, 1), :] * (pt[:, col] - s))
        mixed = jnp.concatenate(mixed, axis=1)
        rate = jnp.dot(rates, mixed, precision=HIGH, preferred_element_type=f32)
        out = mixed + react_step * jnp.tanh(rate)
        e = jnp.dot(forms, out, precision=HIGH, preferred_element_type=f32)
        for j in range(4):
            c = b * 4 + j
            en[pl.ds(c, 1), :] = e[0:1, 128 * j : 128 * j + 128] + kinp[pl.ds(c, 1), :]
            x = out[:, 128 * j : 128 * j + 128]
            col = pl.ds(pl.multiple_of(c * 128, 128), 128)
            rows[col, :] = jnp.concatenate([x, x, x, x], axis=0).T
        return 0

    lax.fori_loop(0, 16, react, 0)
    rows[PD : PD + 8, :] = jnp.zeros((8, 128), f32)
    src_copy.wait()

    def slots(d):
        return ms.at[:, pl.ds(pl.multiple_of(d * CAP, CAP), CAP)]

    def gather_block(p):
        for r in range(128):
            gbuf[r : r + 1, :] = packed(lambda q: src_s[4 * p + q, r])
        t = gbuf[...].T
        for q in range(4):
            sendbuf[p, :, 128 * q : 128 * q + 128] = t[32 * q : 32 * q + 32, :]

    def data(p, d):
        return remote(sendbuf.at[p], slots(d), dss.at[p], drs.at[d], (p, g))

    def send_data(t, _):
        p = ordered_peer(t, me)
        gather_block(p)
        remote(sendbuf.at[p], slots(me), dss.at[p], drs.at[me], (p, g)).start()
        return 0

    lax.fori_loop(0, 16, send_data, 0)

    def bins(b, acc):
        left, right = [], []
        sub = iota((128, 128), 0)
        sub64 = iota((64, 128), 0)
        for j in range(4):
            c = b * 4 + j
            w = cell[pl.ds(c, 1), :]
            m = mass[pl.ds(c, 1), :]
            e = m * en[pl.ds(c, 1), :]
            m_hi = m.astype(bf16).astype(f32)
            e_hi = e.astype(bf16).astype(f32)
            left.append(jnp.where(sub64 == jnp.right_shift(w, 7), 1.0, 0.0).astype(bf16))
            at = sub == jnp.bitwise_and(w, 127)
            right.append(
                jnp.concatenate(
                    [
                        jnp.where(at, y, 0.0).astype(bf16)
                        for y in (e_hi, e - e_hi, m_hi, m - m_hi)
                    ],
                    axis=0,
                )
            )
        return acc + dot_nt(jnp.concatenate(left, axis=1), jnp.concatenate(right, axis=1))

    sums = lax.fori_loop(0, CH // 4, bins, jnp.zeros((64, 512), f32))
    table = jnp.concatenate(
        [sums[:, 0:128] + sums[:, 128:256], sums[:, 256:384] + sums[:, 384:512]], axis=0
    )
    bsend[...] = select_dot(wmat[...], table)
    exchange(bsend, brecv, bss, brs, lsem.at[1])

    lax.fori_loop(16, N - 1, send_data, 0)
    gather_block(me)
    own = pltpu.make_async_copy(sendbuf.at[me], slots(me), lsem.at[5])
    own.start()

    arrive(bsend, brecv, bss, brs, lsem.at[1])
    back = select_dot(q2t[...], brecv[...])
    ce[...] = back[0:64, :]
    cd[...] = back[64:128, :]

    def finish(t, _):
        p = peer(t)
        copy = remote(mbuf.at[p], mm.at[p], mss.at[p], mrs.at[p], (p, g))
        copy.wait_send()
        copy.wait_recv()
        copy = data(p, p)
        copy.wait_send()
        copy.wait_recv()
        return 0

    lax.fori_loop(1, N, finish, 0)
    own_mass.wait()
    own.wait()


def per_device(
    velocity, column_slot, scalars, mass, pair_weight, particle_cell, mix_partner, migrate_to,
    rate_matrix, enthalpy,
):
    slots = column_slot.reshape(1, COLS)
    vrow = jnp.broadcast_to(jnp.concatenate([slots, slots], axis=1), (8, 128))
    vmem = pl.BlockSpec(memory_space=pltpu.VMEM)
    hbm = pl.BlockSpec(memory_space=pl.ANY)
    V = pltpu.VMEM
    D = pltpu.SemaphoreType.DMA
    ce, cd, ms, mm = pl.pallas_call(
        kernel,
        out_shape=(
            jax.ShapeDtypeStruct((64, 128), f32),
            jax.ShapeDtypeStruct((64, 128), f32),
            jax.ShapeDtypeStruct((32, N * CAP), f32),
            jax.ShapeDtypeStruct((N, 4, 128), f32),
        ),
        in_specs=[hbm] * 10,
        out_specs=(vmem, vmem, hbm, hbm),
        scratch_shapes=[
            V((3, 8, 8, 128), f32),
            V((8, 128), i32),
            V((32, PD), f32),
            V((CH, 128), f32),
            V((CH, 128), f32),
            V((CH, 128), i32),
            V((CH, 128), i32),
            V((32, 32), f32),
            V((1, 32), f32),
            V((2, 3, 8, 128), f32),
            V((2, 3, 8, 128), f32),
            V((2, 3, 8, 128), f32),
            V((8, 24, 128), f32),
            V((256, 128), bf16),
            V((128, 256), bf16),
            V((256, 128), bf16),
            V((256, 128), f32),
            V((256, 128), f32),
            V((256, 128), f32),
            V((256, 128), f32),
            V((256, 128), f32),
            V((256, 128), f32),
            V((PD + 8, 128), f32),
            V((32, PD), f32),
            V((128, 128), f32),
            V((CH, 128), i32),
            V((128, 128), i32),
            V((N, 4, 128), f32),
            V((128, 128), f32),
            V((CH, 128), f32),
            V((CH, 128), f32),
            V((CH, 128), f32),
            V((N, 32, CAP), f32),
            pltpu.SMEM((CH, 128), i32),
            pltpu.SMEM((128, 128), i32),
            D((10,)),
            D((6,)),
            D((4,)), D((4,)),
            D((N,)), D((N,)),
            D((N,)), D((N,)),
            D((N,)), D((N,)),
            D((N,)), D((N,)),
            D((N,)), D((N,)),
        ],
        compiler_params=pltpu.CompilerParams(
            collective_id=0, has_side_effects=True, vmem_limit_bytes=60 << 20
        ),
        name="step",
    )(
        velocity,
        vrow,
        scalars,
        mass.reshape(CH, 128),
        pair_weight.reshape(CH, 128),
        particle_cell.reshape(CH, 128),
        migrate_to.reshape(CH, 128),
        mix_partner.reshape(CH, 128),
        rate_matrix,
        enthalpy.reshape(1, 32),
    )
    return (ce.reshape(8, 8, 128), cd.reshape(8, 8, 128), ms, mm.reshape(N * CAP))


def solution(mesh):
    placed = (
        P(None, "flow", "grp", None),
        P("flow", "grp"),
        P(None, ("flow", "grp")),
        P(("flow", "grp")),
        P(("flow", "grp")),
        P(("flow", "grp")),
        P(("flow", "grp")),
        P(("flow", "grp"), None),
        P(),
        P(),
    )
    return jax.shard_map(
        per_device,
        mesh=mesh,
        in_specs=placed,
        out_specs=(
            P("flow", "grp", None),
            P("flow", "grp", None),
            P(None, ("flow", "grp")),
            P(("flow", "grp")),
        ),
        check_vma=False,
    )
```

```python
import functools

import jax
import jax.numpy as jnp
from jax import lax
from jax.experimental import pallas as pl
from jax.experimental.pallas import tpu as pltpu
from jax.sharding import PartitionSpec as P

mix_step = 0.5
react_step = 0.5
MESH = pl.DeviceIdType.MESH
f32 = jnp.float32
bf16 = jnp.bfloat16
i32 = jnp.int32

N = 32
NG = 4
PD = 8192
CH = PD // 128
CAP = 512

_GROUPS = [
    [(2, 2)],
    [(1, 2), (3, 2), (2, 1), (2, 3)],
    [(1, 3), (3, 1)],
    [(1, 1), (3, 3)],
    [(0, 2), (2, 0)],
    [(0, 1), (0, 3), (1, 0), (3, 0)],
]
_ORDER = [(a, b, c) for g in _GROUPS for c in (0, 1) for (a, b) in g] + [
    (0, 0, 1),
    (0, 0, 0),
]
_CODES = [a * 8 + b * 2 + c for (a, b, c) in _ORDER]
_WORDS = [
    sum(code << (5 * j) for j, code in enumerate(_CODES[6 * w : 6 * w + 6]))
    for w in range(6)
]


def ordered_peer(t, me):
    w = t // 6
    word = jnp.int32(_WORDS[0])
    for j in range(1, 6):
        word = jnp.where(w == j, jnp.int32(_WORDS[j]), word)
    code = jnp.bitwise_and(jnp.right_shift(word, 5 * (t - 6 * w)), 31)
    z = lax.rem(me // 8 + code // 8, 4)
    x = lax.rem(lax.rem(me // 2, 4) + lax.rem(code // 2, 4), 4)
    c = lax.rem(me + code, 2)
    return (z * 4 + x) * 2 + c


def split2(x):
    hi = x.astype(bf16)
    lo = (x - hi.astype(f32)).astype(bf16)
    return hi, lo


def split3(x):
    hi = x.astype(bf16)
    r = x - hi.astype(f32)
    mid = r.astype(bf16)
    lo = (r - mid.astype(f32)).astype(bf16)
    return hi, mid, lo


def dot(a, b):
    return jnp.dot(a, b, preferred_element_type=f32)


def dot_nt(a, b):
    return lax.dot_general(a, b, (((1,), (1,)), ((), ())), preferred_element_type=f32)


def select_dot(hot, x):
    a, b, c = split3(x)
    return dot(hot, a) + dot(hot, b) + dot(hot, c)


def iota(shape, dim):
    return lax.broadcasted_iota(i32, shape, dim)


def kernel(
    vel_in, vmap_in, scal_in, mass_in, pw_in, cell_in, mig_in, part, rmat_in, enth_in,
    ce, cd, ms, mm,
    vel, vmap, scal, mass, pw, cell, mig, rmat, enth,
    hx, hy, ysnd, ypad, q2, q2t, wmat, possend, posrecv, fsend, frecv, bsend, brecv,
    rows, pt, gbuf, slot, srcv, partv, iacc, bacc, mbuf, tab, frac, kinp, sendbuf,
    idx_s,
    isem, lsem, xsem, hss, hrs, pss, prs, css, crs, mss, mrs, dss, drs, bss, brs,
):
    me = lax.axis_index("flow")
    g = lax.axis_index("grp")

    def peer(t):
        return lax.rem(me + t, N)

    loads = [
        pltpu.make_async_copy(src, dst, isem.at[k])
        for k, (src, dst) in enumerate(
            [
                (vmap_in, vmap), (vel_in, vel), (scal_in, scal), (mig_in, mig), (mass_in, mass),
                (pw_in, pw), (cell_in, cell), (rmat_in, rmat), (enth_in, enth), (part, partv),
            ]
        )
    ]
    for copy in loads:
        copy.start()

    def remote(src, dst, ss, rs, dev):
        return pltpu.make_async_remote_copy(
            src_ref=src, dst_ref=dst, send_sem=ss, recv_sem=rs, device_id=dev, device_id_type=MESH
        )

    barrier = pltpu.get_barrier_semaphore()

    def greet(t, _):
        pl.semaphore_signal(barrier, inc=1, device_id=(peer(t), g), device_id_type=MESH)
        return 0

    lax.fori_loop(1, N, greet, 0)
    for s in (1, NG - 1):
        pl.semaphore_signal(
            barrier, inc=1, device_id=(me, lax.rem(g + s, NG)), device_id_type=MESH
        )
    loads[0].wait()

    lane1 = iota((1, 128), 1)
    field = jnp.right_shift(lane1, 6)
    spread = jnp.where(
        jnp.bitwise_and(iota((8, 128), 1), 7) == iota((8, 128), 0), 1.0, 0.0
    )
    own_row = jnp.bitwise_and(jnp.right_shift(iota((8, 128), 1), 3), 7) == iota((8, 128), 0)

    def as_row(x):
        wide = jnp.dot(x.astype(f32), spread, preferred_element_type=f32)
        return jnp.sum(jnp.where(own_row, wide, 0.0), axis=0, keepdims=True).astype(i32)

    target = as_row(jnp.right_shift(vmap[...], 6))
    place = as_row(jnp.bitwise_and(vmap[...], 63)) + 64 * field
    key = jnp.broadcast_to((target + 64 * field).astype(f32), (128, 128))
    earlier = jnp.where(
        jnp.logical_and(key.T == key, iota((128, 128), 0) < iota((128, 128), 1)), 1.0, 0.0
    )
    rank = jnp.sum(earlier, axis=0, keepdims=True).astype(i32)
    sidx = target * 8 + field * 4 + rank
    q2v = jnp.where(iota((256, 128), 0) == sidx, 1.0, 0.0).astype(bf16)
    q2[...] = q2v
    sidx_t = jnp.broadcast_to(sidx.astype(f32), (128, 128)).T.astype(i32)
    for h in range(2):
        q2t[:, 128 * h : 128 * h + 128] = jnp.where(
            iota((128, 128), 1) + 128 * h == sidx_t, 1.0, 0.0
        ).astype(bf16)
    place_t = jnp.broadcast_to((place + 1).astype(f32), (128, 128)).T.astype(bf16)
    possend[...] = dot(q2v, place_t) - 1.0
    loads[1].wait()
    for c in range(3):
        for x in range(8):
            ysnd[0, c, x : x + 1, :] = vel[c, x, 0:1, :]
            ysnd[1, c, x : x + 1, :] = vel[c, x, 7:8, :]

    def to_rows(c, _):
        col = pl.ds(pl.multiple_of(c * 128, 128), 128)
        x = scal[:, col]
        rows[col, :] = jnp.concatenate([x, x, x, x], axis=0).T
        return 0

    loads[2].wait()
    lax.fori_loop(0, CH, to_rows, 0, unroll=8)

    pl.semaphore_wait(barrier, N - 1 + 2)

    nxt, prv = lax.rem(me + 1, N), lax.rem(me + N - 1, N)
    gn, gp = lax.rem(g + 1, NG), lax.rem(g + NG - 1, NG)
    halo = [
        remote(vel.at[:, 7], hx.at[0], hss.at[0], hrs.at[0], (nxt, g)),
        remote(vel.at[:, 0], hx.at[1], hss.at[1], hrs.at[1], (prv, g)),
        remote(ysnd.at[1], hy.at[0], hss.at[2], hrs.at[2], (me, gn)),
        remote(ysnd.at[0], hy.at[1], hss.at[3], hrs.at[3], (me, gp)),
    ]
    for copy in halo:
        copy.start()

    def rows8(d):
        return pl.ds(pl.multiple_of(d * 8, 8), 8)

    def exchange(src, dst, ss, rs, own):
        def send(t, _):
            p = peer(t)
            remote(src.at[rows8(p)], dst.at[rows8(me)], ss.at[p], rs.at[me], (p, g)).start()
            return 0

        lax.fori_loop(1, N, send, 0)
        pltpu.make_async_copy(src.at[rows8(me)], dst.at[rows8(me)], own).start()

    def arrive(src, dst, ss, rs, own):
        def done(t, _):
            p = peer(t)
            copy = remote(src.at[rows8(p)], dst.at[rows8(p)], ss.at[p], rs.at[p], (p, g))
            copy.wait_send()
            copy.wait_recv()
            return 0

        lax.fori_loop(1, N, done, 0)
        pltpu.make_async_copy(src.at[rows8(me)], dst.at[rows8(me)], own).wait()

    exchange(possend, posrecv, pss, prs, lsem.at[1])

    for copy in loads[3:9]:
        copy.wait()

    tri = jnp.concatenate(
        [
            jnp.where(iota((128, 128), 0) < iota((128, 128), 1), 1.0, 0.0).astype(bf16),
            jnp.ones((128, 128), bf16),
        ],
        axis=1,
    )

    def ranks(b, carry):
        hots = []
        for j in range(8):
            p = mig[pl.ds(b * 8 + j, 1), :]
            hots.append(jnp.where(iota((32, 128), 0) == p, 1.0, 0.0))
        hot = jnp.concatenate(hots, axis=0)
        pre = dot(hot.astype(bf16), tri)
        out = []
        for j in range(8):
            sl = slice(32 * j, 32 * j + 32)
            out.append(
                jnp.sum(hots[j] * (pre[sl, :128] + carry), axis=0, keepdims=True).astype(i32)
            )
            carry = carry + pre[sl, 128:]
        r8 = pl.ds(pl.multiple_of(b * 8, 8), 8)
        slot[r8, :] = mig[r8, :] * CAP + jnp.concatenate(out, axis=0)
        return carry

    lax.fori_loop(0, 8, ranks, jnp.zeros((32, 128), f32))

    for copy in halo:
        copy.wait()
    strain = jnp.zeros((64, 128), f32)
    square = jnp.zeros((64, 128), f32)
    lane64 = iota((64, 128), 1)
    for c in range(3):
        a = vel[c]
        left = jnp.where(me == 0, 0.0, hx[0, c])
        right = jnp.where(me == N - 1, 0.0, hx[1, c])
        down = jnp.where(g == 0, 0.0, hy[0, c])
        up = jnp.where(g == NG - 1, 0.0, hy[1, c])
        dx = jnp.concatenate([a[1:], right[None]], axis=0) - jnp.concatenate(
            [left[None], a[:-1]], axis=0
        )
        for x in range(8):
            ypad[x, 7:8, :] = down[x : x + 1, :]
            ypad[x, 8:16, :] = a[x]
            ypad[x, 16:17, :] = up[x : x + 1, :]
        dy = ypad[:, 9:17, :] - ypad[:, 7:15, :]
        flat = a.reshape(64, 128)
        dz = jnp.where(lane64 == 127, 0.0, pltpu.roll(flat, 127, 1)) - jnp.where(
            lane64 == 0, 0.0, pltpu.roll(flat, 1, 1)
        )
        dx = dx.reshape(64, 128)
        dy = dy.reshape(64, 128)
        strain = strain + (dx * dx + dy * dy + dz * dz)
        square = square + flat * flat
    omega = 0.5 + 0.25 * jnp.sqrt(strain * 0.25)
    both = jnp.concatenate([omega, 0.5 * square], axis=0)
    fsend[...] = select_dot(q2[...], both)
    exchange(fsend, frecv, css, crs, lsem.at[2])

    def inverse(b):
        left, right = [], []
        sub = iota((128, 128), 0)
        for j in range(4):
            c = b * 4 + j
            s = slot[pl.ds(c, 1), :]
            m = mass[pl.ds(c, 1), :]
            m_hi = m.astype(bf16).astype(f32)
            m_lo = m - m_hi
            left.append(jnp.where(sub == jnp.right_shift(s, 7), 1.0, 0.0).astype(bf16))
            at = sub == jnp.bitwise_and(s, 127)
            code = PD - c * 128 - lane1
            hi = jnp.right_shift(code, 7).astype(f32)
            lo = jnp.bitwise_and(code, 127).astype(f32)
            right.append(
                jnp.concatenate(
                    [jnp.where(at, w, 0.0).astype(bf16) for w in (hi, lo, m_hi, m_lo)], axis=0
                )
            )
        iacc[...] += dot_nt(jnp.concatenate(left, axis=1), jnp.concatenate(right, axis=1))

    lanes = iota((1, 128), 1)
    quarter = [lanes < 32, lanes < 64, lanes < 96]

    def fetch(src, k):
        return pltpu.make_async_copy(src, idx_s.at[k], xsem.at[k])

    def gather(k):
        for r in range(128):
            a, b, c, d = [rows[pl.ds(idx_s[k, q, r], 1), :] for q in range(4)]
            gbuf[k, r : r + 1, :] = jnp.where(
                quarter[1], jnp.where(quarter[0], a, b), jnp.where(quarter[2], c, d)
            )
        return gbuf[k].T

    loads[9].wait()
    for k in range(2):
        fetch(partv.at[k], k).start()
    iacc[...] = jnp.zeros((128, 512), f32)
    bacc[...] = jnp.zeros((64, 512), f32)

    def partners(i, _):
        for k in range(2):
            b = 2 * i + k
            fetch(partv.at[b], k).wait()
            t = gather(k)
            fetch(partv.at[jnp.minimum(b + 2, 14 + k)], k).start()
            for q in range(4):
                col = pl.ds(pl.multiple_of(b * 512 + q * 128, 128), 128)
                pt[:, col] = t[32 * q : 32 * q + 32, :]
            inverse(b)
        return 0

    lax.fori_loop(0, 8, partners, 0)
    for k in range(2):
        fetch(partv.at[14 + k], k).wait()

    inv = iacc[...]
    source = jnp.clip((PD - (inv[:, 0:128] * 128.0 + inv[:, 128:256])).astype(i32), 0, PD)
    moved = inv[:, 256:384] + inv[:, 384:512]
    for p in range(N):
        srcv[p] = source[4 * p : 4 * p + 4, :]
        mbuf[p] = moved[4 * p : 4 * p + 4, :]

    def send_mass(t, _):
        p = peer(t)
        remote(mbuf.at[p], mm.at[me], mss.at[p], mrs.at[me], (p, g)).start()
        return 0

    lax.fori_loop(1, N, send_mass, 0)
    own_mass = pltpu.make_async_copy(mbuf.at[me], mm.at[me], lsem.at[4])
    own_mass.start()

    arrive(possend, posrecv, pss, prs, lsem.at[1])
    pos = posrecv[...]
    wmat[...] = jnp.where(pos == iota((256, 128), 1).astype(f32), 1.0, 0.0).astype(bf16)
    wt = jnp.where(pos.T == iota((128, 256), 0).astype(f32), 1.0, 0.0).astype(bf16)
    arrive(fsend, frecv, css, crs, lsem.at[2])
    tab[...] = select_dot(wt, frecv[...])

    cz = [jnp.bitwise_and(cell[8 * k : 8 * k + 8, :], 127) for k in range(8)]
    cp = [jnp.right_shift(cell[8 * k : 8 * k + 8, :], 7) for k in range(8)]

    def lookup(n, acc):
        om = jnp.broadcast_to(tab[pl.ds(n, 1), :], (8, 128))
        ki = jnp.broadcast_to(tab[pl.ds(n + 64, 1), :], (8, 128))
        out = []
        for k in range(8):
            here = cp[k] == n
            out.append(jnp.where(here, jnp.take_along_axis(om, cz[k], axis=1), acc[2 * k]))
            out.append(jnp.where(here, jnp.take_along_axis(ki, cz[k], axis=1), acc[2 * k + 1]))
        return tuple(out)

    found = lax.fori_loop(0, 64, lookup, tuple(jnp.zeros((8, 128), f32) for _ in range(16)))
    for k in range(8):
        sl = slice(8 * k, 8 * k + 8)
        frac[sl, :] = 1.0 - jnp.exp(-mix_step * pw[sl, :] * found[2 * k])
        kinp[sl, :] = found[2 * k + 1]

    for k in range(2):
        fetch(srcv.at[ordered_peer(k, me)], k).start()

    r_hi = rmat[...].astype(bf16)
    r_lo = (rmat[...] - r_hi.astype(f32)).astype(bf16)
    rates = jnp.concatenate([r_hi, r_hi, r_lo], axis=1)
    f_hi = jnp.broadcast_to(enth[...], (8, 32)).astype(bf16)
    f_lo = (jnp.broadcast_to(enth[...], (8, 32)) - f_hi.astype(f32)).astype(bf16)
    forms = jnp.concatenate([f_hi, f_hi, f_lo], axis=1)

    def react(b, _):
        mixed = []
        for j in range(4):
            c = b * 4 + j
            col = pl.ds(pl.multiple_of(c * 128, 128), 128)
            s = scal[:, col]
            mixed.append(s + frac[pl.ds(c, 1), :] * (pt[:, col] - s))
        mixed = jnp.concatenate(mixed, axis=1)
        hi, lo = split2(mixed)
        out = mixed + react_step * jnp.tanh(dot(rates, jnp.concatenate([hi, lo, hi], axis=0)))
        pt[:, pl.ds(pl.multiple_of(b * 512, 512), 512)] = out
        for j in range(4):
            x = out[:, 128 * j : 128 * j + 128]
            col = pl.ds(pl.multiple_of(b * 512 + j * 128, 128), 128)
            rows[col, :] = jnp.concatenate([x, x, x, x], axis=0).T
        return 0

    lax.fori_loop(0, 16, react, 0, unroll=2)
    rows[PD : PD + 8, :] = jnp.zeros((8, 128), f32)

    def slots(d):
        return ms.at[:, pl.ds(pl.multiple_of(d * CAP, CAP), CAP)]

    def data(p, d):
        return remote(sendbuf.at[p], slots(d), dss.at[p], drs.at[d], (p, g))

    def bins(b):
        left, right = [], []
        sub = iota((128, 128), 0)
        sub64 = iota((64, 128), 0)
        out = pt[:, pl.ds(pl.multiple_of(b * 512, 512), 512)]
        hi, lo = split2(out)
        es = dot(forms, jnp.concatenate([hi, lo, hi], axis=0))
        for j in range(4):
            c = b * 4 + j
            w = cell[pl.ds(c, 1), :]
            m = mass[pl.ds(c, 1), :]
            e = m * (es[0:1, 128 * j : 128 * j + 128] + kinp[pl.ds(c, 1), :])
            m_hi = m.astype(bf16).astype(f32)
            e_hi = e.astype(bf16).astype(f32)
            left.append(jnp.where(sub64 == jnp.right_shift(w, 7), 1.0, 0.0).astype(bf16))
            at = sub == jnp.bitwise_and(w, 127)
            right.append(
                jnp.concatenate(
                    [
                        jnp.where(at, y, 0.0).astype(bf16)
                        for y in (e_hi, e - e_hi, m_hi, m - m_hi)
                    ],
                    axis=0,
                )
            )
        bacc[...] += dot_nt(jnp.concatenate(left, axis=1), jnp.concatenate(right, axis=1))

    def send_pair(i, with_bins):
        for k in range(2):
            t = 2 * i + k
            p = ordered_peer(t, me)
            fetch(srcv.at[p], k).wait()
            block = gather(k)
            fetch(srcv.at[ordered_peer(jnp.minimum(t + 2, 30 + k), me)], k).start()
            for q in range(4):
                sendbuf[p, :, 128 * q : 128 * q + 128] = block[32 * q : 32 * q + 32, :]
            if with_bins:
                bins(t)

            @pl.when(t < N - 1)
            def _():
                remote(sendbuf.at[p], slots(me), dss.at[p], drs.at[me], (p, g)).start()

        return 0

    lax.fori_loop(0, 8, lambda i, _: send_pair(i, True), 0)
    sums = bacc[...]
    table = jnp.concatenate(
        [sums[:, 0:128] + sums[:, 128:256], sums[:, 256:384] + sums[:, 384:512]], axis=0
    )
    bsend[...] = select_dot(wmat[...], table)
    exchange(bsend, brecv, bss, brs, lsem.at[1])
    lax.fori_loop(8, 16, lambda i, _: send_pair(i, False), 0)
    for k in range(2):
        fetch(srcv.at[ordered_peer(30 + k, me)], k).wait()
    own = pltpu.make_async_copy(sendbuf.at[me], slots(me), lsem.at[5])
    own.start()

    arrive(bsend, brecv, bss, brs, lsem.at[1])
    back = select_dot(q2t[...], brecv[...])
    ce[...] = back[0:64, :]
    cd[...] = back[64:128, :]

    def finish(t, _):
        p = peer(t)
        copy = remote(mbuf.at[p], mm.at[p], mss.at[p], mrs.at[p], (p, g))
        copy.wait_send()
        copy.wait_recv()
        copy = data(p, p)
        copy.wait_send()
        copy.wait_recv()
        return 0

    lax.fori_loop(1, N, finish, 0)
    own_mass.wait()
    own.wait()


def write_out(*refs):
    sems = refs[8]
    copies = [pltpu.make_async_copy(refs[k], refs[k + 4], sems.at[k]) for k in (2, 3, 0, 1)]
    for copy in copies:
        copy.start()
    for copy in copies:
        copy.wait()


def per_device(
    velocity, column_slot, scalars, mass, pair_weight, particle_cell, mix_partner, migrate_to,
    rate_matrix, enthalpy,
):
    vmem = pl.BlockSpec(memory_space=pltpu.VMEM)
    hbm = pl.BlockSpec(memory_space=pltpu.HBM)
    anywhere = pl.BlockSpec(memory_space=pl.ANY)
    V = pltpu.VMEM
    D = pltpu.SemaphoreType.DMA
    ce, cd, ms, mm = pl.pallas_call(
        kernel,
        out_shape=(
            jax.ShapeDtypeStruct((64, 128), f32),
            jax.ShapeDtypeStruct((64, 128), f32),
            jax.ShapeDtypeStruct((32, N * CAP), f32),
            jax.ShapeDtypeStruct((N, 4, 128), f32),
        ),
        in_specs=[hbm] * 10,
        out_specs=(vmem, vmem, vmem, vmem),
        scratch_shapes=[
            V((3, 8, 8, 128), f32),
            V((8, 8), i32),
            V((32, PD), f32),
            V((CH, 128), f32),
            V((CH, 128), f32),
            V((CH, 128), i32),
            V((CH, 128), i32),
            V((32, 32), f32),
            V((1, 32), f32),
            V((2, 3, 8, 128), f32),
            V((2, 3, 8, 128), f32),
            V((2, 3, 8, 128), f32),
            V((8, 24, 128), f32),
            V((256, 128), bf16),
            V((128, 256), bf16),
            V((256, 128), bf16),
            V((256, 128), f32),
            V((256, 128), f32),
            V((256, 128), f32),
            V((256, 128), f32),
            V((256, 128), f32),
            V((256, 128), f32),
            V((PD + 8, 128), f32),
            V((32, PD), f32),
            V((2, 128, 128), f32),
            V((CH, 128), i32),
            V((N, 4, 128), i32),
            V((16, 4, 128), i32),
            V((128, 512), f32),
            V((64, 512), f32),
            V((N, 4, 128), f32),
            V((128, 128), f32),
            V((CH, 128), f32),
            V((CH, 128), f32),
            V((N, 32, CAP), f32),
            pltpu.SMEM((2, 4, 128), i32),
            D((10,)),
            D((6,)),
            D((2,)),
            D((4,)), D((4,)),
            D((N,)), D((N,)),
            D((N,)), D((N,)),
            D((N,)), D((N,)),
            D((N,)), D((N,)),
            D((N,)), D((N,)),
        ],
        compiler_params=pltpu.CompilerParams(
            collective_id=0, has_side_effects=True, vmem_limit_bytes=24 << 20
        ),
        name="step",
    )(
        *[
            pltpu.with_memory_space_constraint(x, pltpu.HBM)
            for x in (
                velocity,
                column_slot,
                scalars,
                mass.reshape(CH, 128),
                pair_weight.reshape(CH, 128),
                particle_cell.reshape(CH, 128),
                migrate_to.reshape(CH, 128),
                mix_partner.reshape(16, 4, 128),
                rate_matrix,
                enthalpy.reshape(1, 32),
            )
        ]
    )
    ce, cd, ms, mm = pl.pallas_call(
        write_out,
        out_shape=(
            jax.ShapeDtypeStruct((64, 128), f32),
            jax.ShapeDtypeStruct((64, 128), f32),
            jax.ShapeDtypeStruct((32, N * CAP), f32),
            jax.ShapeDtypeStruct((N, 4, 128), f32),
        ),
        in_specs=[vmem] * 4,
        out_specs=(hbm,) * 4,
        scratch_shapes=[D((4,))],
        compiler_params=pltpu.CompilerParams(vmem_limit_bytes=16 << 20),
        name="write_out",
    )(ce, cd, ms, mm)
    return (ce.reshape(8, 8, 128), cd.reshape(8, 8, 128), ms, mm.reshape(N * CAP))


def solution(mesh):
    placed = (
        P(None, "flow", "grp", None),
        P("flow", "grp"),
        P(None, ("flow", "grp")),
        P(("flow", "grp")),
        P(("flow", "grp")),
        P(("flow", "grp")),
        P(("flow", "grp")),
        P(("flow", "grp"), None),
        P(),
        P(),
    )
    return jax.shard_map(
        per_device,
        mesh=mesh,
        in_specs=placed,
        out_specs=(
            P("flow", "grp", None),
            P("flow", "grp", None),
            P(None, ("flow", "grp")),
            P(("flow", "grp")),
        ),
        check_vma=False,
    )
```

```python
import functools

import jax
import jax.numpy as jnp
from jax import lax
from jax.experimental import pallas as pl
from jax.experimental.pallas import tpu as pltpu
from jax.sharding import PartitionSpec as P

mix_step = 0.5
react_step = 0.5
MESH = pl.DeviceIdType.MESH
f32 = jnp.float32
bf16 = jnp.bfloat16
i32 = jnp.int32

N = 32
NG = 4
PD = 8192
CH = PD // 128
CAP = 512

_GROUPS = [
    [(2, 2)],
    [(1, 2), (3, 2), (2, 1), (2, 3)],
    [(1, 3), (3, 1)],
    [(1, 1), (3, 3)],
    [(0, 2), (2, 0)],
    [(0, 1), (0, 3), (1, 0), (3, 0)],
]
_ORDER = [(a, b, c) for g in _GROUPS for c in (0, 1) for (a, b) in g] + [
    (0, 0, 1),
    (0, 0, 0),
]
_CODES = [a * 8 + b * 2 + c for (a, b, c) in _ORDER]
_WORDS = [
    sum(code << (5 * j) for j, code in enumerate(_CODES[6 * w : 6 * w + 6]))
    for w in range(6)
]


def ordered_peer(t, me):
    w = t // 6
    word = jnp.int32(_WORDS[0])
    for j in range(1, 6):
        word = jnp.where(w == j, jnp.int32(_WORDS[j]), word)
    code = jnp.bitwise_and(jnp.right_shift(word, 5 * (t - 6 * w)), 31)
    z = lax.rem(me // 8 + code // 8, 4)
    x = lax.rem(lax.rem(me // 2, 4) + lax.rem(code // 2, 4), 4)
    c = lax.rem(me + code, 2)
    return (z * 4 + x) * 2 + c


def split2(x):
    hi = x.astype(bf16)
    lo = (x - hi.astype(f32)).astype(bf16)
    return hi, lo


def split3(x):
    hi = x.astype(bf16)
    r = x - hi.astype(f32)
    mid = r.astype(bf16)
    lo = (r - mid.astype(f32)).astype(bf16)
    return hi, mid, lo


def dot(a, b):
    return jnp.dot(a, b, preferred_element_type=f32)


def dot_nt(a, b):
    return lax.dot_general(a, b, (((1,), (1,)), ((), ())), preferred_element_type=f32)


def select_dot(hot, x):
    a, b, c = split3(x)
    return dot(hot, a) + dot(hot, b) + dot(hot, c)


def iota(shape, dim):
    return lax.broadcasted_iota(i32, shape, dim)


def kernel(
    vel_in, vmap_in, scal_in, mass_in, pw_in, cell_in, mig_in, part, rmat_in, enth_in,
    ce, cd, ms, mm,
    vel, vmap, scal, mass, pw, cell, mig, rmat, enth,
    hx, hy, ysnd, ypad, q2, q2t, wmat, possend, posrecv, fsend, frecv, bsend, brecv,
    rows, pt, gbuf, slot, srcv, partv, iacc, bacc, mbuf, tab, frac, found, sendbuf,
    idx_s,
    isem, lsem, xsem, hss, hrs, pss, prs, css, crs, mss, mrs, dss, drs, bss, brs,
):
    me = lax.axis_index("flow")
    g = lax.axis_index("grp")

    def peer(t):
        return lax.rem(me + t, N)

    loads = [
        pltpu.make_async_copy(src, dst, isem.at[k])
        for k, (src, dst) in enumerate(
            [
                (vmap_in, vmap), (vel_in, vel), (scal_in, scal), (mig_in, mig), (mass_in, mass),
                (pw_in, pw), (cell_in, cell), (rmat_in, rmat), (enth_in, enth), (part, partv),
            ]
        )
    ]
    for copy in loads:
        copy.start()

    def remote(src, dst, ss, rs, dev):
        return pltpu.make_async_remote_copy(
            src_ref=src, dst_ref=dst, send_sem=ss, recv_sem=rs, device_id=dev, device_id_type=MESH
        )

    barrier = pltpu.get_barrier_semaphore()

    def greet(t, _):
        pl.semaphore_signal(barrier, inc=1, device_id=(peer(t), g), device_id_type=MESH)
        return 0

    lax.fori_loop(1, N, greet, 0)
    for s in (1, NG - 1):
        pl.semaphore_signal(
            barrier, inc=1, device_id=(me, lax.rem(g + s, NG)), device_id_type=MESH
        )
    loads[0].wait()

    lane1 = iota((1, 128), 1)
    field = jnp.right_shift(lane1, 6)
    spread = jnp.where(
        jnp.bitwise_and(iota((8, 128), 1), 7) == iota((8, 128), 0), 1.0, 0.0
    )
    own_row = jnp.bitwise_and(jnp.right_shift(iota((8, 128), 1), 3), 7) == iota((8, 128), 0)

    def as_row(x):
        wide = jnp.dot(x.astype(f32), spread, preferred_element_type=f32)
        return jnp.sum(jnp.where(own_row, wide, 0.0), axis=0, keepdims=True).astype(i32)

    target = as_row(jnp.right_shift(vmap[...], 6))
    place = as_row(jnp.bitwise_and(vmap[...], 63)) + 64 * field
    key = jnp.broadcast_to((target + 64 * field).astype(f32), (128, 128))
    earlier = jnp.where(
        jnp.logical_and(key.T == key, iota((128, 128), 0) < iota((128, 128), 1)), 1.0, 0.0
    )
    rank = jnp.sum(earlier, axis=0, keepdims=True).astype(i32)
    sidx = target * 8 + field * 4 + rank
    q2v = jnp.where(iota((256, 128), 0) == sidx, 1.0, 0.0).astype(bf16)
    q2[...] = q2v
    sidx_t = jnp.broadcast_to(sidx.astype(f32), (128, 128)).T.astype(i32)
    for h in range(2):
        q2t[:, 128 * h : 128 * h + 128] = jnp.where(
            iota((128, 128), 1) + 128 * h == sidx_t, 1.0, 0.0
        ).astype(bf16)
    place_t = jnp.broadcast_to((place + 1).astype(f32), (128, 128)).T.astype(bf16)
    possend[...] = dot(q2v, place_t) - 1.0
    loads[1].wait()
    for c in range(3):
        for x in range(8):
            ysnd[0, c, x : x + 1, :] = vel[c, x, 0:1, :]
            ysnd[1, c, x : x + 1, :] = vel[c, x, 7:8, :]

    pl.semaphore_wait(barrier, N - 1 + 2)

    nxt, prv = lax.rem(me + 1, N), lax.rem(me + N - 1, N)
    gn, gp = lax.rem(g + 1, NG), lax.rem(g + NG - 1, NG)
    halo = [
        remote(vel.at[:, 7], hx.at[0], hss.at[0], hrs.at[0], (nxt, g)),
        remote(vel.at[:, 0], hx.at[1], hss.at[1], hrs.at[1], (prv, g)),
        remote(ysnd.at[1], hy.at[0], hss.at[2], hrs.at[2], (me, gn)),
        remote(ysnd.at[0], hy.at[1], hss.at[3], hrs.at[3], (me, gp)),
    ]
    for copy in halo:
        copy.start()

    def rows8(d):
        return pl.ds(pl.multiple_of(d * 8, 8), 8)

    def exchange(src, dst, ss, rs, own):
        def send(t, _):
            p = peer(t)
            remote(src.at[rows8(p)], dst.at[rows8(me)], ss.at[p], rs.at[me], (p, g)).start()
            return 0

        lax.fori_loop(1, N, send, 0)
        pltpu.make_async_copy(src.at[rows8(me)], dst.at[rows8(me)], own).start()

    def arrive(src, dst, ss, rs, own):
        def done(t, _):
            p = peer(t)
            copy = remote(src.at[rows8(p)], dst.at[rows8(p)], ss.at[p], rs.at[p], (p, g))
            copy.wait_send()
            copy.wait_recv()
            return 0

        lax.fori_loop(1, N, done, 0)
        pltpu.make_async_copy(src.at[rows8(me)], dst.at[rows8(me)], own).wait()

    exchange(possend, posrecv, pss, prs, lsem.at[1])

    for copy in loads[2:]:
        copy.wait()

    tri = jnp.concatenate(
        [
            jnp.where(iota((128, 128), 0) < iota((128, 128), 1), 1.0, 0.0).astype(bf16),
            jnp.ones((128, 128), bf16),
        ],
        axis=1,
    )

    def ranks(b, carry):
        hots = []
        for j in range(8):
            col = pl.ds(pl.multiple_of((b * 8 + j) * 128, 128), 128)
            x = scal[:, col]
            rows[col, :] = jnp.concatenate([x, x, x, x], axis=0).T
            p = mig[pl.ds(b * 8 + j, 1), :]
            hots.append(jnp.where(iota((32, 128), 0) == p, 1.0, 0.0))
        hot = jnp.concatenate(hots, axis=0)
        pre = dot(hot.astype(bf16), tri)
        out = []
        for j in range(8):
            sl = slice(32 * j, 32 * j + 32)
            out.append(
                jnp.sum(hots[j] * (pre[sl, :128] + carry), axis=0, keepdims=True).astype(i32)
            )
            carry = carry + pre[sl, 128:]
        r8 = pl.ds(pl.multiple_of(b * 8, 8), 8)
        slot[r8, :] = mig[r8, :] * CAP + jnp.concatenate(out, axis=0)
        return carry

    lax.fori_loop(0, 8, ranks, jnp.zeros((32, 128), f32))

    for copy in halo:
        copy.wait()
    strain = jnp.zeros((64, 128), f32)
    square = jnp.zeros((64, 128), f32)
    lane64 = iota((64, 128), 1)
    for c in range(3):
        a = vel[c]
        left = jnp.where(me == 0, 0.0, hx[0, c])
        right = jnp.where(me == N - 1, 0.0, hx[1, c])
        down = jnp.where(g == 0, 0.0, hy[0, c])
        up = jnp.where(g == NG - 1, 0.0, hy[1, c])
        dx = jnp.concatenate([a[1:], right[None]], axis=0) - jnp.concatenate(
            [left[None], a[:-1]], axis=0
        )
        for x in range(8):
            ypad[x, 7:8, :] = down[x : x + 1, :]
            ypad[x, 8:16, :] = a[x]
            ypad[x, 16:17, :] = up[x : x + 1, :]
        dy = ypad[:, 9:17, :] - ypad[:, 7:15, :]
        flat = a.reshape(64, 128)
        dz = jnp.where(lane64 == 127, 0.0, pltpu.roll(flat, 127, 1)) - jnp.where(
            lane64 == 0, 0.0, pltpu.roll(flat, 1, 1)
        )
        dx = dx.reshape(64, 128)
        dy = dy.reshape(64, 128)
        strain = strain + (dx * dx + dy * dy + dz * dz)
        square = square + flat * flat
    omega = 0.5 + 0.25 * jnp.sqrt(strain * 0.25)
    both = jnp.concatenate([omega, 0.5 * square], axis=0)
    fsend[...] = select_dot(q2[...], both)
    exchange(fsend, frecv, css, crs, lsem.at[2])

    def inverse(b):
        left, right = [], []
        sub = iota((128, 128), 0)
        for j in range(4):
            c = b * 4 + j
            s = slot[pl.ds(c, 1), :]
            m = mass[pl.ds(c, 1), :]
            m_hi = m.astype(bf16).astype(f32)
            m_lo = m - m_hi
            left.append(jnp.where(sub == jnp.right_shift(s, 7), 1.0, 0.0).astype(bf16))
            at = sub == jnp.bitwise_and(s, 127)
            code = PD - c * 128 - lane1
            hi = jnp.right_shift(code, 7).astype(f32)
            lo = jnp.bitwise_and(code, 127).astype(f32)
            right.append(
                jnp.concatenate(
                    [jnp.where(at, w, 0.0).astype(bf16) for w in (hi, lo, m_hi, m_lo)], axis=0
                )
            )
        iacc[...] += dot_nt(jnp.concatenate(left, axis=1), jnp.concatenate(right, axis=1))

    lanes = iota((1, 128), 1)
    quarter = [lanes < 32, lanes < 64, lanes < 96]

    def fetch(src, k):
        return pltpu.make_async_copy(src, idx_s.at[k], xsem.at[k])

    def gather(k):
        for r in range(128):
            a, b, c, d = [rows[pl.ds(idx_s[k, q, r], 1), :] for q in range(4)]
            gbuf[k, r : r + 1, :] = jnp.where(
                quarter[1], jnp.where(quarter[0], a, b), jnp.where(quarter[2], c, d)
            )

    for k in range(2):
        fetch(partv.at[k], k).start()
    iacc[...] = jnp.zeros((128, 512), f32)
    bacc[...] = jnp.zeros((64, 512), f32)

    def put_partners(b, t):
        for q in range(4):
            col = pl.ds(pl.multiple_of(b * 512 + q * 128, 128), 128)
            pt[:, col] = t[32 * q : 32 * q + 32, :]

    def lookup(n0):
        acc = [found[8 * k : 8 * k + 8, :] for k in range(16)]
        for j in range(8):
            om = jnp.broadcast_to(tab[pl.ds(n0 + j, 1), :], (8, 128))
            ki = jnp.broadcast_to(tab[pl.ds(n0 + j + 64, 1), :], (8, 128))
            for k in range(8):
                w = cell[8 * k : 8 * k + 8, :]
                z = jnp.bitwise_and(w, 127)
                here = jnp.right_shift(w, 7) == n0 + j
                acc[k] = jnp.where(here, jnp.take_along_axis(om, z, axis=1), acc[k])
                acc[8 + k] = jnp.where(here, jnp.take_along_axis(ki, z, axis=1), acc[8 + k])
        for k in range(16):
            found[8 * k : 8 * k + 8, :] = acc[k]

    def partners(i, with_lookup):
        for k in range(2):
            b = 2 * i + k
            fetch(partv.at[b], k).wait()
            before = gbuf[1 - k].T
            gather(k)
            put_partners(jnp.maximum(b - 1, 0), before)
            inverse(b)
            if with_lookup:
                lookup(8 * (b - 8))
            fetch(partv.at[jnp.minimum(b + 2, 14 + k)], k).start()
        return 0

    lax.fori_loop(0, 4, lambda i, _: partners(i, False), 0)

    arrive(possend, posrecv, pss, prs, lsem.at[1])
    pos = posrecv[...]
    wmat[...] = jnp.where(pos == iota((256, 128), 1).astype(f32), 1.0, 0.0).astype(bf16)
    wt = jnp.where(pos.T == iota((128, 256), 0).astype(f32), 1.0, 0.0).astype(bf16)
    arrive(fsend, frecv, css, crs, lsem.at[2])
    tab[...] = select_dot(wt, frecv[...])
    found[...] = jnp.zeros((128, 128), f32)

    lax.fori_loop(4, 8, lambda i, _: partners(i, True), 0)
    for k in range(2):
        fetch(partv.at[14 + k], k).wait()
    put_partners(15, gbuf[1].T)

    inv = iacc[...]
    source = jnp.clip((PD - (inv[:, 0:128] * 128.0 + inv[:, 128:256])).astype(i32), 0, PD)
    moved = inv[:, 256:384] + inv[:, 384:512]
    for p in range(N):
        srcv[p] = source[4 * p : 4 * p + 4, :]
        mbuf[p] = moved[4 * p : 4 * p + 4, :]

    def send_mass(t, _):
        p = peer(t)
        remote(mbuf.at[p], mm.at[me], mss.at[p], mrs.at[me], (p, g)).start()
        return 0

    lax.fori_loop(1, N, send_mass, 0)
    own_mass = pltpu.make_async_copy(mbuf.at[me], mm.at[me], lsem.at[4])
    own_mass.start()

    frac[...] = 1.0 - jnp.exp(-mix_step * pw[...] * found[0:64, :])

    for k in range(2):
        fetch(srcv.at[ordered_peer(k, me)], k).start()

    r_hi = rmat[...].astype(bf16)
    r_lo = (rmat[...] - r_hi.astype(f32)).astype(bf16)
    rates = jnp.concatenate([r_hi, r_hi, r_lo], axis=1)
    f_hi = jnp.broadcast_to(enth[...], (8, 32)).astype(bf16)
    f_lo = (jnp.broadcast_to(enth[...], (8, 32)) - f_hi.astype(f32)).astype(bf16)
    forms = jnp.concatenate([f_hi, f_hi, f_lo], axis=1)

    def react(b, _):
        mixed = []
        for j in range(4):
            c = b * 4 + j
            col = pl.ds(pl.multiple_of(c * 128, 128), 128)
            s = scal[:, col]
            mixed.append(s + frac[pl.ds(c, 1), :] * (pt[:, col] - s))
        mixed = jnp.concatenate(mixed, axis=1)
        hi, lo = split2(mixed)
        out = mixed + react_step * jnp.tanh(dot(rates, jnp.concatenate([hi, lo, hi], axis=0)))
        pt[:, pl.ds(pl.multiple_of(b * 512, 512), 512)] = out
        for j in range(4):
            x = out[:, 128 * j : 128 * j + 128]
            col = pl.ds(pl.multiple_of(b * 512 + j * 128, 128), 128)
            rows[col, :] = jnp.concatenate([x, x, x, x], axis=0).T
        return 0

    lax.fori_loop(0, 16, react, 0, unroll=2)
    rows[PD : PD + 8, :] = jnp.zeros((8, 128), f32)

    def slots(d):
        return ms.at[:, pl.ds(pl.multiple_of(d * CAP, CAP), CAP)]

    def data(p, d):
        return remote(sendbuf.at[p], slots(d), dss.at[p], drs.at[d], (p, g))

    def bins(b):
        left, right = [], []
        sub = iota((128, 128), 0)
        sub64 = iota((64, 128), 0)
        out = pt[:, pl.ds(pl.multiple_of(b * 512, 512), 512)]
        hi, lo = split2(out)
        es = dot(forms, jnp.concatenate([hi, lo, hi], axis=0))
        for j in range(4):
            c = b * 4 + j
            w = cell[pl.ds(c, 1), :]
            m = mass[pl.ds(c, 1), :]
            e = m * (es[0:1, 128 * j : 128 * j + 128] + found[pl.ds(64 + c, 1), :])
            m_hi = m.astype(bf16).astype(f32)
            e_hi = e.astype(bf16).astype(f32)
            left.append(jnp.where(sub64 == jnp.right_shift(w, 7), 1.0, 0.0).astype(bf16))
            at = sub == jnp.bitwise_and(w, 127)
            right.append(
                jnp.concatenate(
                    [
                        jnp.where(at, y, 0.0).astype(bf16)
                        for y in (e_hi, e - e_hi, m_hi, m - m_hi)
                    ],
                    axis=0,
                )
            )
        bacc[...] += dot_nt(jnp.concatenate(left, axis=1), jnp.concatenate(right, axis=1))

    def put_block(p, t):
        for q in range(4):
            sendbuf[p, :, 128 * q : 128 * q + 128] = t[32 * q : 32 * q + 32, :]

    def send_pair(i, peers, with_bins):
        last, now, soon = peers
        for k in range(2):
            t = 2 * i + k
            fetch(srcv.at[now], k).wait()
            later = ordered_peer(jnp.minimum(t + 2, N - 1), me)
            before = gbuf[1 - k].T
            gather(k)
            put_block(last, before)
            if with_bins:
                bins(t)
            fetch(srcv.at[later], k).start()

            @pl.when(t > 0)
            def _(last=last):
                remote(sendbuf.at[last], slots(me), dss.at[last], drs.at[me], (last, g)).start()

            last, now, soon = now, soon, later
        return last, now, soon

    first, second = ordered_peer(0, me), ordered_peer(1, me)
    peers = lax.fori_loop(0, 8, lambda i, c: send_pair(i, c, True), (first, first, second))
    sums = bacc[...]
    table = jnp.concatenate(
        [sums[:, 0:128] + sums[:, 128:256], sums[:, 256:384] + sums[:, 384:512]], axis=0
    )
    bsend[...] = select_dot(wmat[...], table)
    exchange(bsend, brecv, bss, brs, lsem.at[1])
    lax.fori_loop(8, 16, lambda i, c: send_pair(i, c, False), peers)
    for k in range(2):
        fetch(srcv.at[me], k).wait()
    put_block(me, gbuf[1].T)
    own = pltpu.make_async_copy(sendbuf.at[me], slots(me), lsem.at[5])
    own.start()

    def masses(t, _):
        p = peer(t)
        copy = remote(mbuf.at[p], mm.at[p], mss.at[p], mrs.at[p], (p, g))
        copy.wait_send()
        copy.wait_recv()
        return 0

    lax.fori_loop(1, N, masses, 0)
    own_mass.wait()
    arrive(bsend, brecv, bss, brs, lsem.at[1])
    back = select_dot(q2t[...], brecv[...])
    ce[...] = back[0:64, :]
    cd[...] = back[64:128, :]

    def finish(t, _):
        p = peer(t)
        copy = data(p, p)
        copy.wait_send()
        copy.wait_recv()
        return 0

    lax.fori_loop(1, N, finish, 0)
    own.wait()


def write_out(*refs):
    sems = refs[8]
    copies = [pltpu.make_async_copy(refs[k], refs[k + 4], sems.at[k]) for k in (2, 3, 0, 1)]
    for copy in copies:
        copy.start()
    for copy in copies:
        copy.wait()


def per_device(
    velocity, column_slot, scalars, mass, pair_weight, particle_cell, mix_partner, migrate_to,
    rate_matrix, enthalpy,
):
    vmem = pl.BlockSpec(memory_space=pltpu.VMEM)
    hbm = pl.BlockSpec(memory_space=pltpu.HBM)
    anywhere = pl.BlockSpec(memory_space=pl.ANY)
    V = pltpu.VMEM
    D = pltpu.SemaphoreType.DMA
    ce, cd, ms, mm = pl.pallas_call(
        kernel,
        out_shape=(
            jax.ShapeDtypeStruct((64, 128), f32),
            jax.ShapeDtypeStruct((64, 128), f32),
            jax.ShapeDtypeStruct((32, N * CAP), f32),
            jax.ShapeDtypeStruct((N, 4, 128), f32),
        ),
        in_specs=[hbm] * 10,
        out_specs=(vmem, vmem, vmem, vmem),
        scratch_shapes=[
            V((3, 8, 8, 128), f32),
            V((8, 8), i32),
            V((32, PD), f32),
            V((CH, 128), f32),
            V((CH, 128), f32),
            V((CH, 128), i32),
            V((CH, 128), i32),
            V((32, 32), f32),
            V((1, 32), f32),
            V((2, 3, 8, 128), f32),
            V((2, 3, 8, 128), f32),
            V((2, 3, 8, 128), f32),
            V((8, 24, 128), f32),
            V((256, 128), bf16),
            V((128, 256), bf16),
            V((256, 128), bf16),
            V((256, 128), f32),
            V((256, 128), f32),
            V((256, 128), f32),
            V((256, 128), f32),
            V((256, 128), f32),
            V((256, 128), f32),
            V((PD + 8, 128), f32),
            V((32, PD), f32),
            V((2, 128, 128), f32),
            V((CH, 128), i32),
            V((N, 4, 128), i32),
            V((16, 4, 128), i32),
            V((128, 512), f32),
            V((64, 512), f32),
            V((N, 4, 128), f32),
            V((128, 128), f32),
            V((CH, 128), f32),
            V((128, 128), f32),
            V((N, 32, CAP), f32),
            pltpu.SMEM((2, 4, 128), i32),
            D((10,)),
            D((6,)),
            D((2,)),
            D((4,)), D((4,)),
            D((N,)), D((N,)),
            D((N,)), D((N,)),
            D((N,)), D((N,)),
            D((N,)), D((N,)),
            D((N,)), D((N,)),
        ],
        compiler_params=pltpu.CompilerParams(
            collective_id=0, has_side_effects=True, vmem_limit_bytes=24 << 20
        ),
        name="step",
    )(
        *[
            pltpu.with_memory_space_constraint(x, pltpu.HBM)
            for x in (
                velocity,
                column_slot,
                scalars,
                mass.reshape(CH, 128),
                pair_weight.reshape(CH, 128),
                particle_cell.reshape(CH, 128),
                migrate_to.reshape(CH, 128),
                mix_partner.reshape(16, 4, 128),
                rate_matrix,
                enthalpy.reshape(1, 32),
            )
        ]
    )
    ce, cd, ms, mm = pl.pallas_call(
        write_out,
        out_shape=(
            jax.ShapeDtypeStruct((64, 128), f32),
            jax.ShapeDtypeStruct((64, 128), f32),
            jax.ShapeDtypeStruct((32, N * CAP), f32),
            jax.ShapeDtypeStruct((N, 4, 128), f32),
        ),
        in_specs=[vmem] * 4,
        out_specs=(hbm,) * 4,
        scratch_shapes=[D((4,))],
        compiler_params=pltpu.CompilerParams(vmem_limit_bytes=16 << 20),
        name="write_out",
    )(ce, cd, ms, mm)
    return (ce.reshape(8, 8, 128), cd.reshape(8, 8, 128), ms, mm.reshape(N * CAP))


def solution(mesh):
    placed = (
        P(None, "flow", "grp", None),
        P("flow", "grp"),
        P(None, ("flow", "grp")),
        P(("flow", "grp")),
        P(("flow", "grp")),
        P(("flow", "grp")),
        P(("flow", "grp")),
        P(("flow", "grp"), None),
        P(),
        P(),
    )
    return jax.shard_map(
        per_device,
        mesh=mesh,
        in_specs=placed,
        out_specs=(
            P("flow", "grp", None),
            P("flow", "grp", None),
            P(None, ("flow", "grp")),
            P(("flow", "grp")),
        ),
        check_vma=False,
    )
```

```python
import functools

import jax
import jax.numpy as jnp
from jax import lax
from jax.experimental import pallas as pl
from jax.experimental.pallas import tpu as pltpu
from jax.sharding import PartitionSpec as P

mix_step = 0.5
react_step = 0.5
MESH = pl.DeviceIdType.MESH
f32 = jnp.float32
bf16 = jnp.bfloat16
i32 = jnp.int32

N = 32
NG = 4
PD = 8192
CH = PD // 128
CAP = 512

_GROUPS = [
    [(2, 2)],
    [(1, 2), (3, 2), (2, 1), (2, 3)],
    [(1, 3), (3, 1)],
    [(1, 1), (3, 3)],
    [(0, 2), (2, 0)],
    [(0, 1), (0, 3), (1, 0), (3, 0)],
]
_ORDER = [(a, b, c) for g in _GROUPS for c in (0, 1) for (a, b) in g] + [
    (0, 0, 1),
    (0, 0, 0),
]
_CODES = [a * 8 + b * 2 + c for (a, b, c) in _ORDER]
_WORDS = [
    sum(code << (5 * j) for j, code in enumerate(_CODES[6 * w : 6 * w + 6]))
    for w in range(6)
]


def ordered_peer(t, me):
    w = t // 6
    word = jnp.int32(_WORDS[0])
    for j in range(1, 6):
        word = jnp.where(w == j, jnp.int32(_WORDS[j]), word)
    code = jnp.bitwise_and(jnp.right_shift(word, 5 * (t - 6 * w)), 31)
    z = lax.rem(me // 8 + code // 8, 4)
    x = lax.rem(lax.rem(me // 2, 4) + lax.rem(code // 2, 4), 4)
    c = lax.rem(me + code, 2)
    return (z * 4 + x) * 2 + c


def split2(x):
    hi = x.astype(bf16)
    lo = (x - hi.astype(f32)).astype(bf16)
    return hi, lo


def split3(x):
    hi = x.astype(bf16)
    r = x - hi.astype(f32)
    mid = r.astype(bf16)
    lo = (r - mid.astype(f32)).astype(bf16)
    return hi, mid, lo


def dot(a, b):
    return jnp.dot(a, b, preferred_element_type=f32)


def dot_nt(a, b):
    return lax.dot_general(a, b, (((1,), (1,)), ((), ())), preferred_element_type=f32)


def select_dot(hot, x):
    a, b, c = split3(x)
    return dot(hot, a) + dot(hot, b) + dot(hot, c)


def iota(shape, dim):
    return lax.broadcasted_iota(i32, shape, dim)


def kernel(
    vel_in, vmap_in, scal_in, mass_in, pw_in, cell_in, mig_in, part, rmat_in, enth_in,
    ce, cd, ms, mm,
    vel, vmap, scal, mass, pw, cell, mig, rmat, enth,
    hx, hy, ysnd, ypad, q2, q2t, wmat, possend, posrecv, fsend, frecv, bsend, brecv,
    rows, pt, gbuf, slot, srcv, partv, iacc, sel, bacc, mbuf, tab, frac, found, sendbuf,
    idx_s,
    isem, lsem, xsem, hss, hrs, pss, prs, css, crs, mss, mrs, dss, drs, bss, brs,
):
    me = lax.axis_index("flow")
    g = lax.axis_index("grp")

    def peer(t):
        return lax.rem(me + t, N)

    loads = [
        pltpu.make_async_copy(src, dst, isem.at[k])
        for k, (src, dst) in enumerate(
            [
                (vmap_in, vmap), (vel_in, vel), (scal_in, scal), (mig_in, mig), (mass_in, mass),
                (pw_in, pw), (cell_in, cell), (rmat_in, rmat), (enth_in, enth), (part, partv),
            ]
        )
    ]
    for copy in loads:
        copy.start()

    def remote(src, dst, ss, rs, dev):
        return pltpu.make_async_remote_copy(
            src_ref=src, dst_ref=dst, send_sem=ss, recv_sem=rs, device_id=dev, device_id_type=MESH
        )

    barrier = pltpu.get_barrier_semaphore()

    def greet(t, _):
        pl.semaphore_signal(barrier, inc=1, device_id=(peer(t), g), device_id_type=MESH)
        return 0

    lax.fori_loop(1, N, greet, 0)
    for s in (1, NG - 1):
        pl.semaphore_signal(
            barrier, inc=1, device_id=(me, lax.rem(g + s, NG)), device_id_type=MESH
        )
    loads[0].wait()

    lane1 = iota((1, 128), 1)
    field = jnp.right_shift(lane1, 6)
    spread = jnp.where(
        jnp.bitwise_and(iota((8, 128), 1), 7) == iota((8, 128), 0), 1.0, 0.0
    )
    own_row = jnp.bitwise_and(jnp.right_shift(iota((8, 128), 1), 3), 7) == iota((8, 128), 0)

    def as_row(x):
        wide = jnp.dot(x.astype(f32), spread, preferred_element_type=f32)
        return jnp.sum(jnp.where(own_row, wide, 0.0), axis=0, keepdims=True).astype(i32)

    target = as_row(jnp.right_shift(vmap[...], 6))
    place = as_row(jnp.bitwise_and(vmap[...], 63)) + 64 * field
    key = jnp.broadcast_to((target + 64 * field).astype(f32), (128, 128))
    earlier = jnp.where(
        jnp.logical_and(key.T == key, iota((128, 128), 0) < iota((128, 128), 1)), 1.0, 0.0
    )
    rank = jnp.sum(earlier, axis=0, keepdims=True).astype(i32)
    sidx = target * 8 + field * 4 + rank
    q2v = jnp.where(iota((256, 128), 0) == sidx, 1.0, 0.0).astype(bf16)
    q2[...] = q2v
    sidx_t = jnp.broadcast_to(sidx.astype(f32), (128, 128)).T.astype(i32)
    for h in range(2):
        q2t[:, 128 * h : 128 * h + 128] = jnp.where(
            iota((128, 128), 1) + 128 * h == sidx_t, 1.0, 0.0
        ).astype(bf16)
    place_t = jnp.broadcast_to((place + 1).astype(f32), (128, 128)).T.astype(bf16)
    possend[...] = dot(q2v, place_t) - 1.0
    loads[1].wait()
    for c in range(3):
        for x in range(8):
            ysnd[0, c, x : x + 1, :] = vel[c, x, 0:1, :]
            ysnd[1, c, x : x + 1, :] = vel[c, x, 7:8, :]

    pl.semaphore_wait(barrier, N - 1 + 2)

    nxt, prv = lax.rem(me + 1, N), lax.rem(me + N - 1, N)
    gn, gp = lax.rem(g + 1, NG), lax.rem(g + NG - 1, NG)
    halo = [
        remote(vel.at[:, 7], hx.at[0], hss.at[0], hrs.at[0], (nxt, g)),
        remote(vel.at[:, 0], hx.at[1], hss.at[1], hrs.at[1], (prv, g)),
        remote(ysnd.at[1], hy.at[0], hss.at[2], hrs.at[2], (me, gn)),
        remote(ysnd.at[0], hy.at[1], hss.at[3], hrs.at[3], (me, gp)),
    ]
    for copy in halo:
        copy.start()

    def rows8(d):
        return pl.ds(pl.multiple_of(d * 8, 8), 8)

    def exchange(src, dst, ss, rs, own):
        def send(t, _):
            p = peer(t)
            remote(src.at[rows8(p)], dst.at[rows8(me)], ss.at[p], rs.at[me], (p, g)).start()
            return 0

        lax.fori_loop(1, N, send, 0)
        pltpu.make_async_copy(src.at[rows8(me)], dst.at[rows8(me)], own).start()

    def arrive(src, dst, ss, rs, own):
        def done(t, _):
            p = peer(t)
            copy = remote(src.at[rows8(p)], dst.at[rows8(p)], ss.at[p], rs.at[p], (p, g))
            copy.wait_send()
            copy.wait_recv()
            return 0

        lax.fori_loop(1, N, done, 0)
        pltpu.make_async_copy(src.at[rows8(me)], dst.at[rows8(me)], own).wait()

    exchange(possend, posrecv, pss, prs, lsem.at[1])

    for copy in loads[2:]:
        copy.wait()

    tri = jnp.concatenate(
        [
            jnp.where(iota((128, 128), 0) < iota((128, 128), 1), 1.0, 0.0).astype(bf16),
            jnp.ones((128, 128), bf16),
        ],
        axis=1,
    )

    sel[...] = jnp.where(
        jnp.logical_and(
            jnp.right_shift(jnp.bitwise_and(iota((256, 512), 0), 127), 5)
            == jnp.right_shift(iota((256, 512), 1), 7),
            jnp.bitwise_and(iota((256, 512), 0), 31) == jnp.bitwise_and(iota((256, 512), 1), 31),
        ),
        1.0,
        0.0,
    ).astype(bf16)

    def spread(b, x):
        turned = [
            jnp.concatenate([x[:, 512 * h + 128 * q : 512 * h + 128 * q + 128] for q in range(4)], 0).T
            for h in range(2)
        ]
        out = dot(jnp.concatenate(split2(jnp.concatenate(turned, axis=0)), axis=1), sel[...])
        for h in range(2):
            for q in range(4):
                at = pl.ds(pl.multiple_of(b * 1024 + 512 * h + 128 * q, 128), 128)
                rows[at, :] = out[128 * h : 128 * h + 128, 128 * q : 128 * q + 128]

    def ranks(b, carry):
        spread(b, scal[:, pl.ds(pl.multiple_of(b * 1024, 1024), 1024)])
        hots = []
        for j in range(8):
            p = mig[pl.ds(b * 8 + j, 1), :]
            hots.append(jnp.where(iota((32, 128), 0) == p, 1.0, 0.0))
        hot = jnp.concatenate(hots, axis=0)
        pre = dot(hot.astype(bf16), tri)
        out = []
        for j in range(8):
            sl = slice(32 * j, 32 * j + 32)
            out.append(
                jnp.sum(hots[j] * (pre[sl, :128] + carry), axis=0, keepdims=True).astype(i32)
            )
            carry = carry + pre[sl, 128:]
        r8 = pl.ds(pl.multiple_of(b * 8, 8), 8)
        slot[r8, :] = mig[r8, :] * CAP + jnp.concatenate(out, axis=0)
        return carry

    lax.fori_loop(0, 8, ranks, jnp.zeros((32, 128), f32), unroll=2)

    for copy in halo:
        copy.wait()
    strain = jnp.zeros((64, 128), f32)
    square = jnp.zeros((64, 128), f32)
    lane64 = iota((64, 128), 1)
    for c in range(3):
        a = vel[c]
        left = jnp.where(me == 0, 0.0, hx[0, c])
        right = jnp.where(me == N - 1, 0.0, hx[1, c])
        down = jnp.where(g == 0, 0.0, hy[0, c])
        up = jnp.where(g == NG - 1, 0.0, hy[1, c])
        dx = jnp.concatenate([a[1:], right[None]], axis=0) - jnp.concatenate(
            [left[None], a[:-1]], axis=0
        )
        for x in range(8):
            ypad[x, 7:8, :] = down[x : x + 1, :]
            ypad[x, 8:16, :] = a[x]
            ypad[x, 16:17, :] = up[x : x + 1, :]
        dy = ypad[:, 9:17, :] - ypad[:, 7:15, :]
        flat = a.reshape(64, 128)
        dz = jnp.where(lane64 == 127, 0.0, pltpu.roll(flat, 127, 1)) - jnp.where(
            lane64 == 0, 0.0, pltpu.roll(flat, 1, 1)
        )
        dx = dx.reshape(64, 128)
        dy = dy.reshape(64, 128)
        strain = strain + (dx * dx + dy * dy + dz * dz)
        square = square + flat * flat
    omega = 0.5 + 0.25 * jnp.sqrt(strain * 0.25)
    both = jnp.concatenate([omega, 0.5 * square], axis=0)
    fsend[...] = select_dot(q2[...], both)
    exchange(fsend, frecv, css, crs, lsem.at[2])

    def inverse(b):
        left, right = [], []
        sub = iota((128, 128), 0)
        for j in range(4):
            c = b * 4 + j
            s = slot[pl.ds(c, 1), :]
            m = mass[pl.ds(c, 1), :]
            m_hi = m.astype(bf16).astype(f32)
            m_lo = m - m_hi
            left.append(jnp.where(sub == jnp.right_shift(s, 7), 1.0, 0.0).astype(bf16))
            at = sub == jnp.bitwise_and(s, 127)
            code = PD - c * 128 - lane1
            hi = jnp.right_shift(code, 7).astype(f32)
            lo = jnp.bitwise_and(code, 127).astype(f32)
            right.append(
                jnp.concatenate(
                    [jnp.where(at, w, 0.0).astype(bf16) for w in (hi, lo, m_hi, m_lo)], axis=0
                )
            )
        iacc[...] += dot_nt(jnp.concatenate(left, axis=1), jnp.concatenate(right, axis=1))

    lanes = iota((1, 128), 1)
    quarter = [lanes < 32, lanes < 64, lanes < 96]

    def fetch(src, k):
        return pltpu.make_async_copy(src, idx_s.at[k], xsem.at[k])

    def gather(k):
        for r in range(128):
            a, b, c, d = [rows[pl.ds(idx_s[k, q, r], 1), :] for q in range(4)]
            gbuf[k, r : r + 1, :] = jnp.where(
                quarter[1], jnp.where(quarter[0], a, b), jnp.where(quarter[2], c, d)
            )

    for k in range(2):
        fetch(partv.at[k], k).start()
    iacc[...] = jnp.zeros((128, 512), f32)
    bacc[...] = jnp.zeros((64, 512), f32)

    def put_partners(b, t):
        for q in range(4):
            col = pl.ds(pl.multiple_of(b * 512 + q * 128, 128), 128)
            pt[:, col] = t[32 * q : 32 * q + 32, :]

    def lookup(n0):
        acc = [found[8 * k : 8 * k + 8, :] for k in range(16)]
        for j in range(8):
            om = jnp.broadcast_to(tab[pl.ds(n0 + j, 1), :], (8, 128))
            ki = jnp.broadcast_to(tab[pl.ds(n0 + j + 64, 1), :], (8, 128))
            for k in range(8):
                w = cell[8 * k : 8 * k + 8, :]
                z = jnp.bitwise_and(w, 127)
                here = jnp.right_shift(w, 7) == n0 + j
                acc[k] = jnp.where(here, jnp.take_along_axis(om, z, axis=1), acc[k])
                acc[8 + k] = jnp.where(here, jnp.take_along_axis(ki, z, axis=1), acc[8 + k])
        for k in range(16):
            found[8 * k : 8 * k + 8, :] = acc[k]

    def partners(i, with_lookup):
        for k in range(2):
            b = 2 * i + k
            fetch(partv.at[b], k).wait()
            gather(k)
            fetch(partv.at[jnp.minimum(b + 2, 14 + k)], k).start()
            put_partners(b, gbuf[k].T)
            inverse(b)
            if with_lookup:
                lookup(8 * (b - 8))
        return 0

    lax.fori_loop(0, 4, lambda i, _: partners(i, False), 0)

    arrive(possend, posrecv, pss, prs, lsem.at[1])
    pos = posrecv[...]
    wmat[...] = jnp.where(pos == iota((256, 128), 1).astype(f32), 1.0, 0.0).astype(bf16)
    wt = jnp.where(pos.T == iota((128, 256), 0).astype(f32), 1.0, 0.0).astype(bf16)
    arrive(fsend, frecv, css, crs, lsem.at[2])
    tab[...] = select_dot(wt, frecv[...])
    found[...] = jnp.zeros((128, 128), f32)

    lax.fori_loop(4, 8, lambda i, _: partners(i, True), 0)
    for k in range(2):
        fetch(partv.at[14 + k], k).wait()

    inv = iacc[...]
    source = jnp.clip((PD - (inv[:, 0:128] * 128.0 + inv[:, 128:256])).astype(i32), 0, PD)
    moved = inv[:, 256:384] + inv[:, 384:512]
    for p in range(N):
        srcv[p] = source[4 * p : 4 * p + 4, :]
        mbuf[p] = moved[4 * p : 4 * p + 4, :]

    def send_mass(t, _):
        p = peer(t)
        remote(mbuf.at[p], mm.at[me], mss.at[p], mrs.at[me], (p, g)).start()
        return 0

    lax.fori_loop(1, N, send_mass, 0)
    own_mass = pltpu.make_async_copy(mbuf.at[me], mm.at[me], lsem.at[4])
    own_mass.start()

    frac[...] = 1.0 - jnp.exp(-mix_step * pw[...] * found[0:64, :])

    for k in range(2):
        fetch(srcv.at[ordered_peer(k, me)], k).start()

    r_hi = rmat[...].astype(bf16)
    r_lo = (rmat[...] - r_hi.astype(f32)).astype(bf16)
    rates = jnp.concatenate([r_hi, r_hi, r_lo], axis=1)
    f_hi = jnp.broadcast_to(enth[...], (8, 32)).astype(bf16)
    f_lo = (jnp.broadcast_to(enth[...], (8, 32)) - f_hi.astype(f32)).astype(bf16)
    forms = jnp.concatenate([f_hi, f_hi, f_lo], axis=1)

    def react(b, _):
        mixed = []
        for j in range(8):
            c = b * 8 + j
            col = pl.ds(pl.multiple_of(c * 128, 128), 128)
            s = scal[:, col]
            mixed.append(s + frac[pl.ds(c, 1), :] * (pt[:, col] - s))
        mixed = jnp.concatenate(mixed, axis=1)
        hi, lo = split2(mixed)
        out = mixed + react_step * jnp.tanh(dot(rates, jnp.concatenate([hi, lo, hi], axis=0)))
        pt[:, pl.ds(pl.multiple_of(b * 1024, 1024), 1024)] = out
        spread(b, out)
        return 0

    lax.fori_loop(0, 8, react, 0, unroll=2)
    rows[PD : PD + 8, :] = jnp.zeros((8, 128), f32)

    def slots(d):
        return ms.at[:, pl.ds(pl.multiple_of(d * CAP, CAP), CAP)]

    def data(p, d):
        return remote(sendbuf.at[p], slots(d), dss.at[p], drs.at[d], (p, g))

    def bins(b):
        left, right = [], []
        sub = iota((128, 128), 0)
        sub64 = iota((64, 128), 0)
        out = pt[:, pl.ds(pl.multiple_of(b * 512, 512), 512)]
        hi, lo = split2(out)
        es = dot(forms, jnp.concatenate([hi, lo, hi], axis=0))
        for j in range(4):
            c = b * 4 + j
            w = cell[pl.ds(c, 1), :]
            m = mass[pl.ds(c, 1), :]
            e = m * (es[0:1, 128 * j : 128 * j + 128] + found[pl.ds(64 + c, 1), :])
            m_hi = m.astype(bf16).astype(f32)
            e_hi = e.astype(bf16).astype(f32)
            left.append(jnp.where(sub64 == jnp.right_shift(w, 7), 1.0, 0.0).astype(bf16))
            at = sub == jnp.bitwise_and(w, 127)
            right.append(
                jnp.concatenate(
                    [
                        jnp.where(at, y, 0.0).astype(bf16)
                        for y in (e_hi, e - e_hi, m_hi, m - m_hi)
                    ],
                    axis=0,
                )
            )
        bacc[...] += dot_nt(jnp.concatenate(left, axis=1), jnp.concatenate(right, axis=1))

    def put_block(p, t):
        for q in range(4):
            sendbuf[p, :, 128 * q : 128 * q + 128] = t[32 * q : 32 * q + 32, :]

    def send_pair(i, peers, with_bins):
        last, now, soon = peers
        for k in range(2):
            t = 2 * i + k
            fetch(srcv.at[now], k).wait()
            later = ordered_peer(jnp.minimum(t + 2, N - 1), me)
            before = gbuf[1 - k].T
            gather(k)
            put_block(last, before)
            if with_bins:
                bins(t)
            fetch(srcv.at[later], k).start()

            @pl.when(t > 0)
            def _(last=last):
                remote(sendbuf.at[last], slots(me), dss.at[last], drs.at[me], (last, g)).start()

            last, now, soon = now, soon, later
        return last, now, soon

    first, second = ordered_peer(0, me), ordered_peer(1, me)
    peers = lax.fori_loop(0, 8, lambda i, c: send_pair(i, c, True), (first, first, second))
    sums = bacc[...]
    table = jnp.concatenate(
        [sums[:, 0:128] + sums[:, 128:256], sums[:, 256:384] + sums[:, 384:512]], axis=0
    )
    bsend[...] = select_dot(wmat[...], table)
    exchange(bsend, brecv, bss, brs, lsem.at[1])
    lax.fori_loop(8, 16, lambda i, c: send_pair(i, c, False), peers)
    for k in range(2):
        fetch(srcv.at[me], k).wait()
    put_block(me, gbuf[1].T)
    own = pltpu.make_async_copy(sendbuf.at[me], slots(me), lsem.at[5])
    own.start()

    def masses(t, _):
        p = peer(t)
        copy = remote(mbuf.at[p], mm.at[p], mss.at[p], mrs.at[p], (p, g))
        copy.wait_send()
        copy.wait_recv()
        return 0

    lax.fori_loop(1, N, masses, 0)
    own_mass.wait()
    arrive(bsend, brecv, bss, brs, lsem.at[1])
    back = select_dot(q2t[...], brecv[...])
    ce[...] = back[0:64, :]
    cd[...] = back[64:128, :]

    def finish(t, _):
        p = peer(t)
        copy = data(p, p)
        copy.wait_send()
        copy.wait_recv()
        return 0

    lax.fori_loop(1, N, finish, 0)
    own.wait()


def write_out(*refs):
    sems = refs[8]
    copies = [pltpu.make_async_copy(refs[k], refs[k + 4], sems.at[k]) for k in (2, 3, 0, 1)]
    for copy in copies:
        copy.start()
    for copy in copies:
        copy.wait()


def per_device(
    velocity, column_slot, scalars, mass, pair_weight, particle_cell, mix_partner, migrate_to,
    rate_matrix, enthalpy,
):
    vmem = pl.BlockSpec(memory_space=pltpu.VMEM)
    hbm = pl.BlockSpec(memory_space=pltpu.HBM)
    anywhere = pl.BlockSpec(memory_space=pl.ANY)
    V = pltpu.VMEM
    D = pltpu.SemaphoreType.DMA
    ce, cd, ms, mm = pl.pallas_call(
        kernel,
        out_shape=(
            jax.ShapeDtypeStruct((64, 128), f32),
            jax.ShapeDtypeStruct((64, 128), f32),
            jax.ShapeDtypeStruct((32, N * CAP), f32),
            jax.ShapeDtypeStruct((N, 4, 128), f32),
        ),
        in_specs=[hbm] * 10,
        out_specs=(vmem, vmem, vmem, vmem),
        scratch_shapes=[
            V((3, 8, 8, 128), f32),
            V((8, 8), i32),
            V((32, PD), f32),
            V((CH, 128), f32),
            V((CH, 128), f32),
            V((CH, 128), i32),
            V((CH, 128), i32),
            V((32, 32), f32),
            V((1, 32), f32),
            V((2, 3, 8, 128), f32),
            V((2, 3, 8, 128), f32),
            V((2, 3, 8, 128), f32),
            V((8, 24, 128), f32),
            V((256, 128), bf16),
            V((128, 256), bf16),
            V((256, 128), bf16),
            V((256, 128), f32),
            V((256, 128), f32),
            V((256, 128), f32),
            V((256, 128), f32),
            V((256, 128), f32),
            V((256, 128), f32),
            V((PD + 8, 128), f32),
            V((32, PD), f32),
            V((2, 128, 128), f32),
            V((CH, 128), i32),
            V((N, 4, 128), i32),
            V((16, 4, 128), i32),
            V((128, 512), f32),
            V((256, 512), bf16),
            V((64, 512), f32),
            V((N, 4, 128), f32),
            V((128, 128), f32),
            V((CH, 128), f32),
            V((128, 128), f32),
            V((N, 32, CAP), f32),
            pltpu.SMEM((2, 4, 128), i32),
            D((10,)),
            D((6,)),
            D((2,)),
            D((4,)), D((4,)),
            D((N,)), D((N,)),
            D((N,)), D((N,)),
            D((N,)), D((N,)),
            D((N,)), D((N,)),
            D((N,)), D((N,)),
        ],
        compiler_params=pltpu.CompilerParams(
            collective_id=0, has_side_effects=True, vmem_limit_bytes=24 << 20
        ),
        name="step",
    )(
        *[
            pltpu.with_memory_space_constraint(x, pltpu.HBM)
            for x in (
                velocity,
                column_slot,
                scalars,
                mass.reshape(CH, 128),
                pair_weight.reshape(CH, 128),
                particle_cell.reshape(CH, 128),
                migrate_to.reshape(CH, 128),
                mix_partner.reshape(16, 4, 128),
                rate_matrix,
                enthalpy.reshape(1, 32),
            )
        ]
    )
    ce, cd, ms, mm = pl.pallas_call(
        write_out,
        out_shape=(
            jax.ShapeDtypeStruct((64, 128), f32),
            jax.ShapeDtypeStruct((64, 128), f32),
            jax.ShapeDtypeStruct((32, N * CAP), f32),
            jax.ShapeDtypeStruct((N, 4, 128), f32),
        ),
        in_specs=[vmem] * 4,
        out_specs=(hbm,) * 4,
        scratch_shapes=[D((4,))],
        compiler_params=pltpu.CompilerParams(vmem_limit_bytes=16 << 20),
        name="write_out",
    )(ce, cd, ms, mm)
    return (ce.reshape(8, 8, 128), cd.reshape(8, 8, 128), ms, mm.reshape(N * CAP))


def solution(mesh):
    placed = (
        P(None, "flow", "grp", None),
        P("flow", "grp"),
        P(None, ("flow", "grp")),
        P(("flow", "grp")),
        P(("flow", "grp")),
        P(("flow", "grp")),
        P(("flow", "grp")),
        P(("flow", "grp"), None),
        P(),
        P(),
    )
    return jax.shard_map(
        per_device,
        mesh=mesh,
        in_specs=placed,
        out_specs=(
            P("flow", "grp", None),
            P("flow", "grp", None),
            P(None, ("flow", "grp")),
            P(("flow", "grp")),
        ),
        check_vma=False,
    )
```

```python
import functools

import jax
import jax.numpy as jnp
from jax import lax
from jax.experimental import pallas as pl
from jax.experimental.pallas import tpu as pltpu
from jax.sharding import PartitionSpec as P

mix_step = 0.5
react_step = 0.5
MESH = pl.DeviceIdType.MESH
f32 = jnp.float32
bf16 = jnp.bfloat16
i32 = jnp.int32

N = 32
NG = 4
PD = 8192
CH = PD // 128
CAP = 512

_GROUPS = [
    [(2, 2)],
    [(1, 2), (3, 2), (2, 1), (2, 3)],
    [(1, 3), (3, 1)],
    [(1, 1), (3, 3)],
    [(0, 2), (2, 0)],
    [(0, 1), (0, 3), (1, 0), (3, 0)],
]
_ORDER = [(a, b, c) for g in _GROUPS for c in (0, 1) for (a, b) in g] + [
    (0, 0, 1),
    (0, 0, 0),
]
_CODES = [a * 8 + b * 2 + c for (a, b, c) in _ORDER]
_WORDS = [
    sum(code << (5 * j) for j, code in enumerate(_CODES[6 * w : 6 * w + 6]))
    for w in range(6)
]


def ordered_peer(t, me):
    w = t // 6
    word = jnp.int32(_WORDS[0])
    for j in range(1, 6):
        word = jnp.where(w == j, jnp.int32(_WORDS[j]), word)
    code = jnp.bitwise_and(jnp.right_shift(word, 5 * (t - 6 * w)), 31)
    z = lax.rem(me // 8 + code // 8, 4)
    x = lax.rem(lax.rem(me // 2, 4) + lax.rem(code // 2, 4), 4)
    c = lax.rem(me + code, 2)
    return (z * 4 + x) * 2 + c


def split2(x):
    hi = x.astype(bf16)
    lo = (x - hi.astype(f32)).astype(bf16)
    return hi, lo


def split3(x):
    hi = x.astype(bf16)
    r = x - hi.astype(f32)
    mid = r.astype(bf16)
    lo = (r - mid.astype(f32)).astype(bf16)
    return hi, mid, lo


def dot(a, b):
    return jnp.dot(a, b, preferred_element_type=f32)


def dot_nt(a, b):
    return lax.dot_general(a, b, (((1,), (1,)), ((), ())), preferred_element_type=f32)


def select_dot(hot, x):
    a, b, c = split3(x)
    return dot(hot, a) + dot(hot, b) + dot(hot, c)


def iota(shape, dim):
    return lax.broadcasted_iota(i32, shape, dim)


def kernel(
    vel_in, vmap_in, scal_in, mass_in, pw_in, cell_in, mig_in, part, rmat_in, enth_in,
    ce, cd, ms, mm,
    vel, vmap, scal, mass, pw, cell, mig, rmat, enth,
    hx, hy, ysnd, ypad, q2, q2t, wmat, possend, posrecv, fsend, frecv, bsend, brecv,
    rows, pt, gbuf, slot, srcv, partv, iacc, sel, bacc, mbuf, tab, frac, found, sendbuf,
    idx_s,
    isem, lsem, xsem, hss, hrs, pss, prs, css, crs, mss, mrs, dss, drs, bss, brs,
):
    me = lax.axis_index("flow")
    g = lax.axis_index("grp")

    def peer(t):
        return lax.rem(me + t, N)

    loads = [
        pltpu.make_async_copy(src, dst, isem.at[k])
        for k, (src, dst) in enumerate(
            [
                (vmap_in, vmap), (vel_in, vel), (scal_in, scal), (mig_in, mig), (mass_in, mass),
                (pw_in, pw), (cell_in, cell), (rmat_in, rmat), (enth_in, enth), (part, partv),
            ]
        )
    ]
    for copy in loads:
        copy.start()

    def remote(src, dst, ss, rs, dev):
        return pltpu.make_async_remote_copy(
            src_ref=src, dst_ref=dst, send_sem=ss, recv_sem=rs, device_id=dev, device_id_type=MESH
        )

    barrier = pltpu.get_barrier_semaphore()

    def greet(t, _):
        pl.semaphore_signal(barrier, inc=1, device_id=(peer(t), g), device_id_type=MESH)
        return 0

    lax.fori_loop(1, N, greet, 0)
    for s in (1, NG - 1):
        pl.semaphore_signal(
            barrier, inc=1, device_id=(me, lax.rem(g + s, NG)), device_id_type=MESH
        )
    loads[0].wait()

    lane1 = iota((1, 128), 1)
    field = jnp.right_shift(lane1, 6)
    spread = jnp.where(
        jnp.bitwise_and(iota((8, 128), 1), 7) == iota((8, 128), 0), 1.0, 0.0
    )
    own_row = jnp.bitwise_and(jnp.right_shift(iota((8, 128), 1), 3), 7) == iota((8, 128), 0)

    def as_row(x):
        wide = jnp.dot(x.astype(f32), spread, preferred_element_type=f32)
        return jnp.sum(jnp.where(own_row, wide, 0.0), axis=0, keepdims=True).astype(i32)

    target = as_row(jnp.right_shift(vmap[...], 6))
    place = as_row(jnp.bitwise_and(vmap[...], 63)) + 64 * field
    key = jnp.broadcast_to((target + 64 * field).astype(f32), (128, 128))
    earlier = jnp.where(
        jnp.logical_and(key.T == key, iota((128, 128), 0) < iota((128, 128), 1)), 1.0, 0.0
    )
    rank = jnp.sum(earlier, axis=0, keepdims=True).astype(i32)
    sidx = target * 8 + field * 4 + rank
    q2v = jnp.where(iota((256, 128), 0) == sidx, 1.0, 0.0).astype(bf16)
    q2[...] = q2v
    sidx_t = jnp.broadcast_to(sidx.astype(f32), (128, 128)).T.astype(i32)
    for h in range(2):
        q2t[:, 128 * h : 128 * h + 128] = jnp.where(
            iota((128, 128), 1) + 128 * h == sidx_t, 1.0, 0.0
        ).astype(bf16)
    place_t = jnp.broadcast_to((place + 1).astype(f32), (128, 128)).T.astype(bf16)
    possend[...] = dot(q2v, place_t) - 1.0
    loads[1].wait()
    for c in range(3):
        for x in range(8):
            ysnd[0, c, x : x + 1, :] = vel[c, x, 0:1, :]
            ysnd[1, c, x : x + 1, :] = vel[c, x, 7:8, :]

    pl.semaphore_wait(barrier, N - 1 + 2)

    nxt, prv = lax.rem(me + 1, N), lax.rem(me + N - 1, N)
    gn, gp = lax.rem(g + 1, NG), lax.rem(g + NG - 1, NG)
    halo = [
        remote(vel.at[:, 7], hx.at[0], hss.at[0], hrs.at[0], (nxt, g)),
        remote(vel.at[:, 0], hx.at[1], hss.at[1], hrs.at[1], (prv, g)),
        remote(ysnd.at[1], hy.at[0], hss.at[2], hrs.at[2], (me, gn)),
        remote(ysnd.at[0], hy.at[1], hss.at[3], hrs.at[3], (me, gp)),
    ]
    for copy in halo:
        copy.start()

    def rows8(d):
        return pl.ds(pl.multiple_of(d * 8, 8), 8)

    def exchange(src, dst, ss, rs, own):
        def send(t, _):
            p = peer(t)
            remote(src.at[rows8(p)], dst.at[rows8(me)], ss.at[p], rs.at[me], (p, g)).start()
            return 0

        lax.fori_loop(1, N, send, 0)
        pltpu.make_async_copy(src.at[rows8(me)], dst.at[rows8(me)], own).start()

    def arrive(src, dst, ss, rs, own):
        def done(t, _):
            p = peer(t)
            copy = remote(src.at[rows8(p)], dst.at[rows8(p)], ss.at[p], rs.at[p], (p, g))
            copy.wait_send()
            copy.wait_recv()
            return 0

        lax.fori_loop(1, N, done, 0)
        pltpu.make_async_copy(src.at[rows8(me)], dst.at[rows8(me)], own).wait()

    exchange(possend, posrecv, pss, prs, lsem.at[1])

    for copy in loads[2:]:
        copy.wait()

    tri = jnp.concatenate(
        [
            jnp.where(iota((128, 128), 0) < iota((128, 128), 1), 1.0, 0.0).astype(bf16),
            jnp.ones((128, 128), bf16),
        ],
        axis=1,
    )

    sel[...] = jnp.where(
        jnp.logical_and(
            jnp.right_shift(jnp.bitwise_and(iota((256, 512), 0), 127), 5)
            == jnp.right_shift(iota((256, 512), 1), 7),
            jnp.bitwise_and(iota((256, 512), 0), 31) == jnp.bitwise_and(iota((256, 512), 1), 31),
        ),
        1.0,
        0.0,
    ).astype(bf16)

    def spread(b, x):
        turned = [
            jnp.concatenate([x[:, 512 * h + 128 * q : 512 * h + 128 * q + 128] for q in range(4)], 0).T
            for h in range(2)
        ]
        out = dot(jnp.concatenate(split2(jnp.concatenate(turned, axis=0)), axis=1), sel[...])
        for h in range(2):
            for q in range(4):
                at = pl.ds(pl.multiple_of(b * 1024 + 512 * h + 128 * q, 128), 128)
                rows[at, :] = out[128 * h : 128 * h + 128, 128 * q : 128 * q + 128]

    def ranks(b, carry):
        spread(b, scal[:, pl.ds(pl.multiple_of(b * 1024, 1024), 1024)])
        hots = []
        for j in range(8):
            p = mig[pl.ds(b * 8 + j, 1), :]
            hots.append(jnp.where(iota((32, 128), 0) == p, 1.0, 0.0))
        hot = jnp.concatenate(hots, axis=0)
        pre = dot(hot.astype(bf16), tri)
        out = []
        for j in range(8):
            sl = slice(32 * j, 32 * j + 32)
            out.append(
                jnp.sum(hots[j] * (pre[sl, :128] + carry), axis=0, keepdims=True).astype(i32)
            )
            carry = carry + pre[sl, 128:]
        r8 = pl.ds(pl.multiple_of(b * 8, 8), 8)
        slot[r8, :] = mig[r8, :] * CAP + jnp.concatenate(out, axis=0)
        return carry

    lax.fori_loop(0, 8, ranks, jnp.zeros((32, 128), f32), unroll=2)

    for copy in halo:
        copy.wait()
    strain = jnp.zeros((64, 128), f32)
    square = jnp.zeros((64, 128), f32)
    lane64 = iota((64, 128), 1)
    for c in range(3):
        a = vel[c]
        left = jnp.where(me == 0, 0.0, hx[0, c])
        right = jnp.where(me == N - 1, 0.0, hx[1, c])
        down = jnp.where(g == 0, 0.0, hy[0, c])
        up = jnp.where(g == NG - 1, 0.0, hy[1, c])
        dx = jnp.concatenate([a[1:], right[None]], axis=0) - jnp.concatenate(
            [left[None], a[:-1]], axis=0
        )
        for x in range(8):
            ypad[x, 7:8, :] = down[x : x + 1, :]
            ypad[x, 8:16, :] = a[x]
            ypad[x, 16:17, :] = up[x : x + 1, :]
        dy = ypad[:, 9:17, :] - ypad[:, 7:15, :]
        flat = a.reshape(64, 128)
        dz = jnp.where(lane64 == 127, 0.0, pltpu.roll(flat, 127, 1)) - jnp.where(
            lane64 == 0, 0.0, pltpu.roll(flat, 1, 1)
        )
        dx = dx.reshape(64, 128)
        dy = dy.reshape(64, 128)
        strain = strain + (dx * dx + dy * dy + dz * dz)
        square = square + flat * flat
    omega = 0.5 + 0.25 * jnp.sqrt(strain * 0.25)
    both = jnp.concatenate([omega, 0.5 * square], axis=0)
    fsend[...] = select_dot(q2[...], both)
    exchange(fsend, frecv, css, crs, lsem.at[2])

    def inverse(b):
        left, right = [], []
        sub = iota((128, 128), 0)
        for j in range(4):
            c = b * 4 + j
            s = slot[pl.ds(c, 1), :]
            m = mass[pl.ds(c, 1), :]
            m_hi = m.astype(bf16).astype(f32)
            m_lo = m - m_hi
            left.append(jnp.where(sub == jnp.right_shift(s, 7), 1.0, 0.0).astype(bf16))
            at = sub == jnp.bitwise_and(s, 127)
            code = PD - c * 128 - lane1
            hi = jnp.right_shift(code, 7).astype(f32)
            lo = jnp.bitwise_and(code, 127).astype(f32)
            right.append(
                jnp.concatenate(
                    [jnp.where(at, w, 0.0).astype(bf16) for w in (hi, lo, m_hi, m_lo)], axis=0
                )
            )
        iacc[...] += dot_nt(jnp.concatenate(left, axis=1), jnp.concatenate(right, axis=1))

    lanes = iota((1, 128), 1)
    quarter = [lanes < 32, lanes < 64, lanes < 96]

    def fetch(src, k):
        return pltpu.make_async_copy(src, idx_s.at[k], xsem.at[k])

    def gather(k):
        for r in range(128):
            a, b, c, d = [rows[pl.ds(idx_s[k, q, r], 1), :] for q in range(4)]
            gbuf[k, r : r + 1, :] = jnp.where(
                quarter[1], jnp.where(quarter[0], a, b), jnp.where(quarter[2], c, d)
            )

    for k in range(2):
        fetch(partv.at[k], k).start()
    iacc[...] = jnp.zeros((128, 512), f32)
    bacc[...] = jnp.zeros((64, 512), f32)

    def put_partners(b, t):
        for q in range(4):
            col = pl.ds(pl.multiple_of(b * 512 + q * 128, 128), 128)
            pt[:, col] = t[32 * q : 32 * q + 32, :]

    def lookup(n0):
        tables = []
        for j in range(8):
            tables.append(
                [jnp.broadcast_to(tab[pl.ds(n0 + j + f, 1), :], (8, 128)) for f in (0, 64)]
            )
        for k in range(8):
            w = cell[8 * k : 8 * k + 8, :]
            z = jnp.bitwise_and(w, 127)
            n = jnp.right_shift(w, 7) - n0
            acc = [found[8 * k : 8 * k + 8, :], found[64 + 8 * k : 72 + 8 * k, :]]
            for j in range(8):
                here = n == j
                for f in range(2):
                    acc[f] = jnp.where(here, jnp.take_along_axis(tables[j][f], z, axis=1), acc[f])
            found[8 * k : 8 * k + 8, :] = acc[0]
            found[64 + 8 * k : 72 + 8 * k, :] = acc[1]

    def partners(i, with_lookup):
        for k in range(2):
            b = 2 * i + k
            fetch(partv.at[b], k).wait()
            gather(k)
            fetch(partv.at[jnp.minimum(b + 2, 14 + k)], k).start()
            put_partners(b, gbuf[k].T)
            inverse(b)
            if with_lookup:
                lookup(8 * (b - 8))
        return 0

    lax.fori_loop(0, 4, lambda i, _: partners(i, False), 0)

    arrive(possend, posrecv, pss, prs, lsem.at[1])
    pos = posrecv[...]
    wmat[...] = jnp.where(pos == iota((256, 128), 1).astype(f32), 1.0, 0.0).astype(bf16)
    wt = jnp.where(pos.T == iota((128, 256), 0).astype(f32), 1.0, 0.0).astype(bf16)
    arrive(fsend, frecv, css, crs, lsem.at[2])
    tab[...] = select_dot(wt, frecv[...])
    found[...] = jnp.zeros((128, 128), f32)

    lax.fori_loop(4, 8, lambda i, _: partners(i, True), 0)
    for k in range(2):
        fetch(partv.at[14 + k], k).wait()

    inv = iacc[...]
    source = jnp.clip((PD - (inv[:, 0:128] * 128.0 + inv[:, 128:256])).astype(i32), 0, PD)
    for p in range(N):
        srcv[p] = source[4 * p : 4 * p + 4, :]

    frac[...] = 1.0 - jnp.exp(-mix_step * pw[...] * found[0:64, :])

    for k in range(2):
        fetch(srcv.at[ordered_peer(k, me)], k).start()

    r_hi = rmat[...].astype(bf16)
    r_lo = (rmat[...] - r_hi.astype(f32)).astype(bf16)
    rates = jnp.concatenate([r_hi, r_hi, r_lo], axis=1)
    f_hi = jnp.broadcast_to(enth[...], (8, 32)).astype(bf16)
    f_lo = (jnp.broadcast_to(enth[...], (8, 32)) - f_hi.astype(f32)).astype(bf16)
    forms = jnp.concatenate([f_hi, f_hi, f_lo], axis=1)

    def react(b, _):
        mixed = []
        for j in range(8):
            c = b * 8 + j
            col = pl.ds(pl.multiple_of(c * 128, 128), 128)
            s = scal[:, col]
            mixed.append(s + frac[pl.ds(c, 1), :] * (pt[:, col] - s))
        mixed = jnp.concatenate(mixed, axis=1)
        hi, lo = split2(mixed)
        out = mixed + react_step * jnp.tanh(dot(rates, jnp.concatenate([hi, lo, hi], axis=0)))
        pt[:, pl.ds(pl.multiple_of(b * 1024, 1024), 1024)] = out
        spread(b, out)
        return 0

    lax.fori_loop(0, 8, react, 0, unroll=2)
    rows[PD : PD + 8, :] = jnp.zeros((8, 128), f32)

    def slots(d):
        return ms.at[:, pl.ds(pl.multiple_of(d * CAP, CAP), CAP)]

    def data(p, d):
        return remote(sendbuf.at[p], slots(d), dss.at[p], drs.at[d], (p, g))

    def bins(b):
        left, right = [], []
        sub = iota((128, 128), 0)
        sub64 = iota((64, 128), 0)
        out = pt[:, pl.ds(pl.multiple_of(b * 512, 512), 512)]
        hi, lo = split2(out)
        es = dot(forms, jnp.concatenate([hi, lo, hi], axis=0))
        for j in range(4):
            c = b * 4 + j
            w = cell[pl.ds(c, 1), :]
            m = mass[pl.ds(c, 1), :]
            e = m * (es[0:1, 128 * j : 128 * j + 128] + found[pl.ds(64 + c, 1), :])
            m_hi = m.astype(bf16).astype(f32)
            e_hi = e.astype(bf16).astype(f32)
            left.append(jnp.where(sub64 == jnp.right_shift(w, 7), 1.0, 0.0).astype(bf16))
            at = sub == jnp.bitwise_and(w, 127)
            right.append(
                jnp.concatenate(
                    [
                        jnp.where(at, y, 0.0).astype(bf16)
                        for y in (e_hi, e - e_hi, m_hi, m - m_hi)
                    ],
                    axis=0,
                )
            )
        bacc[...] += dot_nt(jnp.concatenate(left, axis=1), jnp.concatenate(right, axis=1))

    def put_block(p, t):
        for q in range(4):
            sendbuf[p, :, 128 * q : 128 * q + 128] = t[32 * q : 32 * q + 32, :]

    def send_pair(i, peers, with_bins):
        last, now, soon = peers
        for k in range(2):
            t = 2 * i + k
            fetch(srcv.at[now], k).wait()
            later = ordered_peer(jnp.minimum(t + 2, N - 1), me)
            before = gbuf[1 - k].T
            gather(k)
            put_block(last, before)
            if with_bins:
                bins(t)
            fetch(srcv.at[later], k).start()

            @pl.when(t > 0)
            def _(last=last):
                remote(sendbuf.at[last], slots(me), dss.at[last], drs.at[me], (last, g)).start()

            last, now, soon = now, soon, later
        return last, now, soon

    first, second = ordered_peer(0, me), ordered_peer(1, me)
    peers = lax.fori_loop(0, 8, lambda i, c: send_pair(i, c, True), (first, first, second))
    sums = bacc[...]
    table = jnp.concatenate(
        [sums[:, 0:128] + sums[:, 128:256], sums[:, 256:384] + sums[:, 384:512]], axis=0
    )
    bsend[...] = select_dot(wmat[...], table)
    exchange(bsend, brecv, bss, brs, lsem.at[1])
    moved = iacc[:, 256:384] + iacc[:, 384:512]
    for p in range(N):
        mbuf[p] = moved[4 * p : 4 * p + 4, :]

    def send_mass(t, _):
        p = peer(t)
        remote(mbuf.at[p], mm.at[me], mss.at[p], mrs.at[me], (p, g)).start()
        return 0

    lax.fori_loop(1, N, send_mass, 0)
    own_mass = pltpu.make_async_copy(mbuf.at[me], mm.at[me], lsem.at[4])
    own_mass.start()

    lax.fori_loop(8, 16, lambda i, c: send_pair(i, c, False), peers)
    for k in range(2):
        fetch(srcv.at[me], k).wait()
    put_block(me, gbuf[1].T)
    own = pltpu.make_async_copy(sendbuf.at[me], slots(me), lsem.at[5])
    own.start()

    def masses(t, _):
        p = peer(t)
        copy = remote(mbuf.at[p], mm.at[p], mss.at[p], mrs.at[p], (p, g))
        copy.wait_send()
        copy.wait_recv()
        return 0

    lax.fori_loop(1, N, masses, 0)
    own_mass.wait()
    arrive(bsend, brecv, bss, brs, lsem.at[1])
    back = select_dot(q2t[...], brecv[...])
    ce[...] = back[0:64, :]
    cd[...] = back[64:128, :]

    def finish(t, _):
        p = peer(t)
        copy = data(p, p)
        copy.wait_send()
        copy.wait_recv()
        return 0

    lax.fori_loop(1, N, finish, 0)
    own.wait()


def write_out(*refs):
    sems = refs[8]
    copies = [pltpu.make_async_copy(refs[k], refs[k + 4], sems.at[k]) for k in (2, 3, 0, 1)]
    for copy in copies:
        copy.start()
    for copy in copies:
        copy.wait()


def per_device(
    velocity, column_slot, scalars, mass, pair_weight, particle_cell, mix_partner, migrate_to,
    rate_matrix, enthalpy,
):
    vmem = pl.BlockSpec(memory_space=pltpu.VMEM)
    hbm = pl.BlockSpec(memory_space=pltpu.HBM)
    anywhere = pl.BlockSpec(memory_space=pl.ANY)
    V = pltpu.VMEM
    D = pltpu.SemaphoreType.DMA
    ce, cd, ms, mm = pl.pallas_call(
        kernel,
        out_shape=(
            jax.ShapeDtypeStruct((64, 128), f32),
            jax.ShapeDtypeStruct((64, 128), f32),
            jax.ShapeDtypeStruct((32, N * CAP), f32),
            jax.ShapeDtypeStruct((N, 4, 128), f32),
        ),
        in_specs=[hbm] * 10,
        out_specs=(vmem, vmem, vmem, vmem),
        scratch_shapes=[
            V((3, 8, 8, 128), f32),
            V((8, 8), i32),
            V((32, PD), f32),
            V((CH, 128), f32),
            V((CH, 128), f32),
            V((CH, 128), i32),
            V((CH, 128), i32),
            V((32, 32), f32),
            V((1, 32), f32),
            V((2, 3, 8, 128), f32),
            V((2, 3, 8, 128), f32),
            V((2, 3, 8, 128), f32),
            V((8, 24, 128), f32),
            V((256, 128), bf16),
            V((128, 256), bf16),
            V((256, 128), bf16),
            V((256, 128), f32),
            V((256, 128), f32),
            V((256, 128), f32),
            V((256, 128), f32),
            V((256, 128), f32),
            V((256, 128), f32),
            V((PD + 8, 128), f32),
            V((32, PD), f32),
            V((2, 128, 128), f32),
            V((CH, 128), i32),
            V((N, 4, 128), i32),
            V((16, 4, 128), i32),
            V((128, 512), f32),
            V((256, 512), bf16),
            V((64, 512), f32),
            V((N, 4, 128), f32),
            V((128, 128), f32),
            V((CH, 128), f32),
            V((128, 128), f32),
            V((N, 32, CAP), f32),
            pltpu.SMEM((2, 4, 128), i32),
            D((10,)),
            D((6,)),
            D((2,)),
            D((4,)), D((4,)),
            D((N,)), D((N,)),
            D((N,)), D((N,)),
            D((N,)), D((N,)),
            D((N,)), D((N,)),
            D((N,)), D((N,)),
        ],
        compiler_params=pltpu.CompilerParams(
            collective_id=0, has_side_effects=True, vmem_limit_bytes=24 << 20
        ),
        name="step",
    )(
        *[
            pltpu.with_memory_space_constraint(x, pltpu.HBM)
            for x in (
                velocity,
                column_slot,
                scalars,
                mass.reshape(CH, 128),
                pair_weight.reshape(CH, 128),
                particle_cell.reshape(CH, 128),
                migrate_to.reshape(CH, 128),
                mix_partner.reshape(16, 4, 128),
                rate_matrix,
                enthalpy.reshape(1, 32),
            )
        ]
    )
    ce, cd, ms, mm = pl.pallas_call(
        write_out,
        out_shape=(
            jax.ShapeDtypeStruct((64, 128), f32),
            jax.ShapeDtypeStruct((64, 128), f32),
            jax.ShapeDtypeStruct((32, N * CAP), f32),
            jax.ShapeDtypeStruct((N, 4, 128), f32),
        ),
        in_specs=[vmem] * 4,
        out_specs=(hbm,) * 4,
        scratch_shapes=[D((4,))],
        compiler_params=pltpu.CompilerParams(vmem_limit_bytes=16 << 20),
        name="write_out",
    )(ce, cd, ms, mm)
    return (ce.reshape(8, 8, 128), cd.reshape(8, 8, 128), ms, mm.reshape(N * CAP))


def solution(mesh):
    placed = (
        P(None, "flow", "grp", None),
        P("flow", "grp"),
        P(None, ("flow", "grp")),
        P(("flow", "grp")),
        P(("flow", "grp")),
        P(("flow", "grp")),
        P(("flow", "grp")),
        P(("flow", "grp"), None),
        P(),
        P(),
    )
    return jax.shard_map(
        per_device,
        mesh=mesh,
        in_specs=placed,
        out_specs=(
            P("flow", "grp", None),
            P("flow", "grp", None),
            P(None, ("flow", "grp")),
            P(("flow", "grp")),
        ),
        check_vma=False,
    )
```
